32 devices in a mesh: group: 2 (over y), hour: 4 (over z), cluster: 2 (over x), mp: 2 (over core).
Axes of the slice: x: 2, y: 2, z: 4, core: 2. Of those that a mesh axis runs over, the one named last changes fastest.
Arguments:
- tokens: bfloat16 [1024, 8, 1024], P(('group', 'hour'), 'cluster'), parts along dimension 0, may hold values from -6 to 6
- cotangent: bfloat16 [1024, 8, 1024], P(('group', 'hour'), 'cluster'), parts along dimension 0, may hold values from -6 to 6
- hour_of: int32 [1024], P('group'), parts along dimension 0, may hold values from 0 to 511, each once
- adjacency: int32 [4, 2], replicated, may hold values from 0 to 3, as said below
- temporal_query_key_value: bfloat16 [3, 1024, 512], P(None, None, 'mp'), may hold values from -0.1875 to 0.1875
- time_out: bfloat16 [512, 1024], P('mp'), may hold values from -0.25 to 0.25
- spatial_query_key_value: bfloat16 [3, 1024, 512], P(None, None, 'mp'), may hold values from -0.1875 to 0.1875
- space_out: bfloat16 [512, 1024], P('mp'), may hold values from -0.25 to 0.25
Outputs:
- grad_tokens: bfloat16 [1024, 8, 1024], P(('group', 'hour'), 'cluster'), parts along dimension 0
The draws below stay inside these ranges and needn't reach their ends.
There are 2 independent parts, one for each index of `group`. The reference program is written for one: setup_inputs(seed, part) draws one part's arguments, and reference() takes and returns one part's arrays. A program takes and returns all parts, laid end to end along the dimension named above; an argument that names none is the same for every part. Nothing has to cross between parts.
Inputs may be any that keep to these rules, and one draw needn't show every extreme that they name: `hour_of`: each hour index appears exactly once. `adjacency`: each row names 2 different blocks.
All inputs are finite; a program needn't handle non-finite values.
Results may differ from the reference program's by a relative error of at most 0.025.
Values may be sent and summed in bfloat16 or wider, within the bound.
A program may use at most 128 MiB of HBM per device.

```python
import jax
import jax.numpy as jnp
from jax import lax

D = 1024
HEADS = 8
HS = 64
SBLK = 2
NSB = 4
KB = 2
H = 512
S = 8


def draw_adjacency(key, part):

    def one_row(index):
        order = jax.random.permutation(jax.random.fold_in(key, index), NSB)
        return order[:KB].astype(jnp.int32)
    return jax.vmap(one_row)(jnp.arange(NSB, dtype=jnp.int32))


def level_of(rng, shape, split, low, high):
    level, own = 1.0, jax.random.fold_in(rng, 6)
    for axis_at, parts in split:
        steps = jnp.exp(jax.random.uniform(jax.random.fold_in(own, axis_at), (parts,), jnp.float32, low / len(split), high / len(split)))
        level = level * jnp.repeat(steps, shape[axis_at] // parts).reshape([-1 if axis == axis_at else 1 for axis in range(len(shape))])
    return level


def noise(own_key, extent, deviation, reach, shards=(), kind=jnp.bfloat16):
    factor_of = level_of(own_key, extent, shards, -0.22, 0.18) if shards else 1.0
    drawn = jax.random.normal(own_key, extent, jnp.float32) * deviation * factor_of
    return jnp.minimum(jnp.maximum(drawn, -reach), reach).astype(kind)


def setup_inputs(seed: int = 0, part: int = 0) -> dict:
    seeds = jax.random.split(jax.random.key(seed), 9)
    part_splits = jax.random.split(jax.random.fold_in(seeds[8], part), 9)
    return {
        "tokens": noise(part_splits[0], (H, S, D), 1.0, 6.0, ((0, 4), (1, 2))),
        "cotangent": noise(part_splits[1], (H, S, D), 1.0, 6.0, ((0, 4), (1, 2))),
        "hour_of": jax.random.permutation(part_splits[2], H).astype(jnp.int32),
        "adjacency": draw_adjacency(jax.random.fold_in(seeds[8], 71), part),
        "temporal_query_key_value": noise(seeds[4], (3, D, HEADS * HS), D ** -0.5, 0.1875, ((2, 2),)),
        "time_out": noise(seeds[5], (HEADS * HS, D), (HEADS * HS) ** -0.5, 0.25, ((0, 2),)),
        "spatial_query_key_value": noise(seeds[6], (3, D, HEADS * HS), D ** -0.5, 0.1875, ((2, 2),)),
        "space_out": noise(seeds[7], (HEADS * HS, D), (HEADS * HS) ** -0.5, 0.25, ((0, 2),)),
    }


EPS_ROW = 1e-05
EPS_HEAD = 1e-06
SCORE_SCALE = 0.25

def rounded_values(values):
    return lax.optimization_barrier(values.astype(jnp.bfloat16))

def row_scale(values, epsilon):
    return lax.rsqrt(lax.optimization_barrier(jnp.mean(values * values, axis=-1, keepdims=True)) + epsilon)

def norm_back(normed, scale, grad):
    return scale * (grad - normed * lax.optimization_barrier(jnp.mean(normed * grad, axis=-1, keepdims=True)))

def split_heads(values):
    return values.reshape(values.shape[:-1] + (HEADS, HS))

def merge_heads(values):
    return values.reshape(values.shape[:-2] + (HEADS * HS,))

def to_units(values):
    return jnp.transpose(values, (1, 2, 0, 3)).reshape(S * HEADS, H, HS)

def from_cluster_units(values):
    return jnp.transpose(values.reshape(S, HEADS, H, HS), (2, 0, 1, 3))

def project_normalised_rows(input_tokens, weights):
    scale = row_scale(input_tokens, EPS_ROW)
    normed = input_tokens * scale
    projected = jnp.einsum('tsd,cdq->ctsq', rounded_values(normed).astype(jnp.float32), weights.astype(jnp.float32))
    query = split_heads(projected[0])
    query_scale = row_scale(query, EPS_HEAD)
    keyed = split_heads(projected[1])
    key_scale = row_scale(keyed, EPS_HEAD)
    values = rounded_values(split_heads(projected[2]))
    return (normed, scale, query * query_scale, query_scale, keyed * key_scale, key_scale, values)

def input_gradient_rows(normed, scale, norm_q, q_scale, norm_k, k_scale, grad_q, grad_k, grad_v, weights):
    query_grad = rounded_values(norm_back(norm_q, q_scale, grad_q))
    key_grad = rounded_values(norm_back(norm_k, k_scale, grad_k))
    stacked = jnp.stack([merge_heads(query_grad), merge_heads(key_grad), merge_heads(grad_v)]).astype(jnp.float32)
    partial_value = jnp.einsum('ctsq,cdq->tsd', stacked, weights.astype(jnp.float32))
    return norm_back(normed, scale, partial_value)

def time_probs(query, keys, visible):
    scores = jnp.dot(query, keys.T, preferred_element_type=jnp.float32) * SCORE_SCALE
    weights = jnp.where(visible, jnp.exp(scores), 0.0)
    return weights / lax.optimization_barrier(jnp.sum(weights, axis=-1, keepdims=True))

def time_forward(query, keys, values, visible):
    probs = time_probs(query, keys, visible)
    return jnp.dot(rounded_values(probs), values, preferred_element_type=jnp.float32).astype(jnp.bfloat16)

def time_backward(query, keys, values, grad_out, visible):
    probs = time_probs(query, keys, visible)
    dprob = jnp.dot(grad_out, values.T, preferred_element_type=jnp.float32)
    delta = lax.optimization_barrier(jnp.sum(probs * dprob, axis=-1, keepdims=True))
    dscore = rounded_values(probs * (dprob - delta) * SCORE_SCALE)
    dquery = jnp.dot(dscore, keys, preferred_element_type=jnp.float32)
    dkey = jnp.dot(dscore.T, query, preferred_element_type=jnp.float32)
    dvalue = jnp.dot(rounded_values(probs).T, grad_out, preferred_element_type=jnp.float32)
    return (dquery, dkey, dvalue)

def reference(tokens, cotangent, hour_of, adjacency, temporal_query_key_value, time_out, spatial_query_key_value, space_out):
    visible = hour_of[None, :] <= hour_of[:, None]
    input_tokens = tokens.astype(jnp.float32)
    temporal_normalised, temporal_scale, temporal_query, temporal_query_scale, temporal_key, temporal_key_scale, temporal_value = project_normalised_rows(input_tokens, temporal_query_key_value)
    query_low = rounded_values(temporal_query)
    key_low = rounded_values(temporal_key)
    attended = lax.map(lambda unit: time_forward(unit[0], unit[1], unit[2], visible), (to_units(query_low), to_units(key_low), to_units(temporal_value)))
    attended = merge_heads(from_cluster_units(attended)).astype(jnp.float32)
    mixed = jnp.einsum('tsq,qd->tsd', attended, time_out.astype(jnp.float32))
    hidden_state = rounded_values(input_tokens + mixed).astype(jnp.float32)
    spatial_normalised, spatial_scale, spatial_query, spatial_query_scale, spatial_key, spatial_key_scale, spatial_value = project_normalised_rows(hidden_state, spatial_query_key_value)
    query_sp = rounded_values(spatial_query).astype(jnp.float32)
    key_sp = rounded_values(spatial_key).astype(jnp.float32)
    value_sp = spatial_value.astype(jnp.float32)
    grad_sp = rounded_values(jnp.einsum('tsd,qd->tsq', cotangent.astype(jnp.float32), space_out.astype(jnp.float32)))
    grad_sp = split_heads(grad_sp).astype(jnp.float32)
    block = jnp.arange(S) // SBLK
    listed = jnp.any(adjacency[:, :, None] == jnp.arange(NSB)[None, None, :], axis=1)
    near = listed[block][:, block]
    scores_two = jnp.einsum('tihd,tjhd->thij', query_sp, key_sp) * SCORE_SCALE
    weights_two = jnp.where(near, jnp.exp(scores_two), 0.0)
    probs_two = weights_two / lax.optimization_barrier(jnp.sum(weights_two, axis=-1, keepdims=True))
    dprob_two = jnp.einsum('tihd,tjhd->thij', grad_sp, value_sp)
    delta_two = lax.optimization_barrier(jnp.sum(probs_two * dprob_two, axis=-1, keepdims=True))
    dscore_two = rounded_values(probs_two * (dprob_two - delta_two) * SCORE_SCALE).astype(jnp.float32)
    spatial_query_gradient = rounded_values(jnp.einsum('thij,tjhd->tihd', dscore_two, key_sp)).astype(jnp.float32)
    spatial_key_gradient = rounded_values(jnp.einsum('thij,tihd->tjhd', dscore_two, query_sp)).astype(jnp.float32)
    spatial_value_gradient = rounded_values(jnp.einsum('thij,tihd->tjhd', rounded_values(probs_two).astype(jnp.float32), grad_sp))
    hidden_state_gradient = cotangent.astype(jnp.float32) + input_gradient_rows(spatial_normalised, spatial_scale, spatial_query, spatial_query_scale, spatial_key, spatial_key_scale, spatial_query_gradient, spatial_key_gradient, spatial_value_gradient, spatial_query_key_value)
    grad_low = rounded_values(hidden_state_gradient).astype(jnp.float32)
    grad_one = rounded_values(split_heads(jnp.einsum('tsd,qd->tsq', grad_low, time_out.astype(jnp.float32))))
    temporal_query_gradient, temporal_key_gradient, temporal_value_gradient = lax.map(lambda unit: time_backward(unit[0], unit[1], unit[2], unit[3], visible), (to_units(query_low), to_units(key_low), to_units(temporal_value), to_units(grad_one)))
    input_gradient_total = input_gradient_rows(temporal_normalised, temporal_scale, temporal_query, temporal_query_scale, temporal_key, temporal_key_scale, from_cluster_units(temporal_query_gradient), from_cluster_units(temporal_key_gradient), rounded_values(from_cluster_units(temporal_value_gradient)), temporal_query_key_value)
    return (hidden_state_gradient + input_gradient_total).astype(jnp.bfloat16)
```

```python
import functools

import jax
import jax.numpy as jnp
from jax import lax
from jax.experimental import pallas as pl
from jax.experimental.pallas import tpu as pltpu
from jax.sharding import PartitionSpec as P

HS = 64
SBLK = 2
NSB = 4
S = 8


EPS_ROW = 1e-05
EPS_HEAD = 1e-06
SCORE_SCALE = 0.25
LOG2E = 1.4426950408889634


def row_scale(values, epsilon):
    return lax.rsqrt(jnp.mean(values * values, axis=-1, keepdims=True) + epsilon)


def norm_back(normed, scale, grad):
    return scale * (grad - normed * jnp.mean(normed * grad, axis=-1, keepdims=True))


def split_heads(values):
    return values.reshape(values.shape[:-1] + (values.shape[-1] // HS, HS))


def merge_heads(values):
    return values.reshape(values.shape[:-2] + (values.shape[-2] * values.shape[-1],))


def head_totals(partial_value):
    return lax.psum(partial_value.astype(jnp.bfloat16), "mp").astype(jnp.float32)


def project_normalised_rows(input_tokens, weights):
    scale = row_scale(input_tokens, EPS_ROW)
    normed = input_tokens * scale
    projected = jnp.einsum(
        "tsd,cdq->ctsq", normed.astype(jnp.bfloat16), weights, preferred_element_type=jnp.float32
    )
    query = split_heads(projected[0])
    query_scale = row_scale(query, EPS_HEAD)
    keyed = split_heads(projected[1])
    key_scale = row_scale(keyed, EPS_HEAD)
    values = split_heads(projected[2]).astype(jnp.bfloat16)
    return (normed, scale, query * query_scale, query_scale, keyed * key_scale, key_scale, values)


def input_gradient_rows(
    normed, scale, norm_q, q_scale, norm_k, k_scale, grad_q, grad_k, grad_v, weights
):
    query_grad = norm_back(norm_q, q_scale, grad_q).astype(jnp.bfloat16)
    key_grad = norm_back(norm_k, k_scale, grad_k).astype(jnp.bfloat16)
    stacked = jnp.stack([merge_heads(query_grad), merge_heads(key_grad), merge_heads(grad_v)])
    partial_value = jnp.einsum(
        "ctsq,cdq->tsd", stacked, weights, preferred_element_type=jnp.float32
    )
    return norm_back(normed, scale, head_totals(partial_value))


def shards(
    tokens,
    cotangent,
    hour_of,
    adjacency,
    temporal_query_key_value,
    time_out,
    spatial_query_key_value,
    space_out,
):
    rows = tokens.shape[0]
    local_hours = lax.dynamic_slice_in_dim(hour_of, lax.axis_index("hour") * rows, rows)
    input_tokens = tokens.astype(jnp.float32)
    (
        temporal_normalised,
        temporal_scale,
        temporal_query,
        temporal_query_scale,
        temporal_key,
        temporal_key_scale,
        temporal_value,
    ) = project_normalised_rows(input_tokens, temporal_query_key_value)
    query_low = temporal_query.astype(jnp.bfloat16)
    key_low = temporal_key.astype(jnp.bfloat16)
    key_all, value_all = (
        lax.all_gather(merge_heads(key_low), "hour", axis=0, tiled=True),
        lax.all_gather(merge_heads(temporal_value), "hour", axis=0, tiled=True),
    )
    key_all = split_heads(key_all)
    value_all = split_heads(value_all)
    visible = hour_of[None, :] <= local_hours[:, None]
    scores = (
        jnp.einsum("ishd,jshd->shij", query_low, key_all, preferred_element_type=jnp.float32)
        * SCORE_SCALE
    )
    weights = jnp.where(visible, jnp.exp(scores), 0.0)
    totals = jnp.sum(weights, axis=-1, keepdims=True)
    probs = weights / totals
    probs_low = probs.astype(jnp.bfloat16)
    attended = jnp.einsum(
        "shij,jshd->ishd", probs_low, value_all, preferred_element_type=jnp.float32
    ).astype(jnp.bfloat16)
    mixed = jnp.einsum(
        "isq,qd->isd", merge_heads(attended), time_out, preferred_element_type=jnp.float32
    )
    hidden_state = lax.optimization_barrier(
        (input_tokens + head_totals(mixed)).astype(jnp.bfloat16)
    ).astype(jnp.float32)
    (
        spatial_normalised,
        spatial_scale,
        spatial_query,
        spatial_query_scale,
        spatial_key,
        spatial_key_scale,
        spatial_value,
    ) = project_normalised_rows(hidden_state, spatial_query_key_value)
    grad_out = jnp.einsum(
        "isd,qd->isq", cotangent, space_out, preferred_element_type=jnp.float32
    ).astype(jnp.bfloat16)
    query_near, key_near, value_near, grad_near = (
        lax.all_to_all(
            merge_heads(spatial_query.astype(jnp.bfloat16)),
            "cluster",
            split_axis=0,
            concat_axis=1,
            tiled=True,
        ),
        lax.all_to_all(
            merge_heads(spatial_key.astype(jnp.bfloat16)),
            "cluster",
            split_axis=0,
            concat_axis=1,
            tiled=True,
        ),
        lax.all_to_all(
            merge_heads(spatial_value), "cluster", split_axis=0, concat_axis=1, tiled=True
        ),
        lax.all_to_all(grad_out, "cluster", split_axis=0, concat_axis=1, tiled=True),
    )
    query_near = split_heads(query_near)
    key_near = split_heads(key_near)
    value_near = split_heads(value_near)
    grad_near = split_heads(grad_near)
    block = jnp.arange(S) // SBLK
    listed = jnp.sum(
        (adjacency[:, :, None] == jnp.arange(NSB)[None, None, :]).astype(jnp.float32), axis=1
    )
    member = (block[:, None] == jnp.arange(NSB)[None, :]).astype(jnp.float32)
    near = jnp.dot(jnp.dot(member, listed), member.T) > 0.5
    scores_two = (
        jnp.einsum("rihd,rjhd->rhij", query_near, key_near, preferred_element_type=jnp.float32)
        * SCORE_SCALE
    )
    weights_two = jnp.where(near, jnp.exp(scores_two), 0.0)
    probs_two = weights_two / jnp.sum(weights_two, axis=-1, keepdims=True)
    dprob_two = jnp.einsum(
        "rihd,rjhd->rhij", grad_near, value_near, preferred_element_type=jnp.float32
    )
    delta_two = jnp.sum(probs_two * dprob_two, axis=-1, keepdims=True)
    dscore_two = (probs_two * (dprob_two - delta_two) * SCORE_SCALE).astype(jnp.bfloat16)
    dquery_near = jnp.einsum(
        "rhij,rjhd->rihd", dscore_two, key_near, preferred_element_type=jnp.float32
    ).astype(jnp.bfloat16)
    dkey_near = jnp.einsum(
        "rhij,rihd->rjhd", dscore_two, query_near, preferred_element_type=jnp.float32
    ).astype(jnp.bfloat16)
    dvalue_near = jnp.einsum(
        "rhij,rihd->rjhd",
        probs_two.astype(jnp.bfloat16),
        grad_near,
        preferred_element_type=jnp.float32,
    ).astype(jnp.bfloat16)
    spatial_query_gradient, spatial_key_gradient, spatial_value_gradient = (
        lax.all_to_all(
            merge_heads(dquery_near), "cluster", split_axis=1, concat_axis=0, tiled=True
        ),
        lax.all_to_all(merge_heads(dkey_near), "cluster", split_axis=1, concat_axis=0, tiled=True),
        lax.all_to_all(
            merge_heads(dvalue_near), "cluster", split_axis=1, concat_axis=0, tiled=True
        ),
    )
    hidden_state_gradient = cotangent.astype(jnp.float32) + input_gradient_rows(
        spatial_normalised,
        spatial_scale,
        spatial_query,
        spatial_query_scale,
        spatial_key,
        spatial_key_scale,
        split_heads(spatial_query_gradient).astype(jnp.float32),
        split_heads(spatial_key_gradient).astype(jnp.float32),
        split_heads(spatial_value_gradient),
        spatial_query_key_value,
    )
    grad_low = hidden_state_gradient.astype(jnp.bfloat16)
    grad_one = split_heads(
        jnp.einsum("isd,qd->isq", grad_low, time_out, preferred_element_type=jnp.float32).astype(
            jnp.bfloat16
        )
    )
    dprob = jnp.einsum("ishd,jshd->shij", grad_one, value_all, preferred_element_type=jnp.float32)
    delta = jnp.sum(probs * dprob, axis=-1, keepdims=True)
    dscore = (probs * (dprob - delta) * SCORE_SCALE).astype(jnp.bfloat16)
    temporal_query_gradient = jnp.einsum(
        "shij,jshd->ishd", dscore, key_all, preferred_element_type=jnp.float32
    )
    key_part = jnp.einsum("shij,ishd->jshd", dscore, query_low, preferred_element_type=jnp.float32)
    value_part = jnp.einsum(
        "shij,ishd->jshd", probs_low, grad_one, preferred_element_type=jnp.float32
    )
    summed = lax.psum_scatter(
        jnp.concatenate([merge_heads(key_part), merge_heads(value_part)], axis=-1).astype(
            jnp.bfloat16
        ),
        "hour",
        scatter_dimension=0,
        tiled=True,
    ).astype(jnp.float32)
    half_width = summed.shape[-1] // 2
    temporal_key_gradient = split_heads(summed[..., :half_width])
    temporal_value_gradient = split_heads(summed[..., half_width:])
    input_gradient_total = input_gradient_rows(
        temporal_normalised,
        temporal_scale,
        temporal_query,
        temporal_query_scale,
        temporal_key,
        temporal_key_scale,
        temporal_query_gradient,
        temporal_key_gradient,
        temporal_value_gradient.astype(jnp.bfloat16),
        temporal_query_key_value,
    )
    return (hidden_state_gradient + input_gradient_total).astype(jnp.bfloat16)


NT = (((1,), (1,)), ((), ()))


def dot(a, b):
    return jnp.dot(a, b, preferred_element_type=jnp.float32)


def dot_nt(a, b):
    return lax.dot_general(a, b, NT, preferred_element_type=jnp.float32)


def low(values):
    return values.astype(jnp.bfloat16)


def layer_kernel(
    cfg,
    tok_in,
    cot_in,
    hour_row,
    adj,
    w1,
    wo1,
    w2,
    wo2,
    out,
    rawt,
    rawc,
    tok,
    cot,
    tokT,
    tokS,
    cotS,
    w1v,
    woF,
    w2F,
    wsF,
    nrm,
    qT1,
    kT1,
    r1q,
    r1k,
    qTb1,
    kb1,
    kTb1,
    vb1,
    vTb1,
    E1,
    li1,
    oT1,
    dqT1,
    dk1,
    dv1,
    o1buf,
    o1S,
    qT2,
    kT2,
    r2T,
    qTb2,
    kb2,
    kTb2,
    vb2,
    gT2,
    dqT2,
    dk2,
    dv2,
    g1buf,
    g1T,
    dhs,
    dhO,
    psend,
    precv,
    pown,
    g3,
    t1s,
    t1O,
    outb,
    loc_sem,
    z_send,
    z_recv,
    f_send,
    f_recv,
    x_send,
    x_recv,
    w_send,
    w_recv,
    o_send,
    o_recv,
    g_send,
    g_recv,
    d_send,
    d_recv,
    p_send,
    p_recv,
    t_send,
    t_recv,
    e_send,
    e_recv,
):
    NH, NC, RW, D, W = cfg
    HL = W // HS
    HB = NC * RW
    BLK = 2 * HB
    NT1 = NH * BLK
    NS = NC * NH
    U = 2
    RU = RW // U
    N2 = NS * RU
    QU = NT1 // U
    hr = lax.axis_index("hour")
    cl = lax.axis_index("cluster")
    m = lax.axis_index("mp")
    sib = 1 - m
    offsets = [
        (a, b, c) for c in range(2) for b in range(NC) for a in range(NH) if (a, b, c) != (0, 0, 0)
    ]

    def peer(off):
        return (lax.rem(hr + off[0], NH), lax.rem(cl + off[1], NC), lax.rem(m + off[2], 2))

    def ids(p):
        return {"hour": p[0], "cluster": p[1], "mp": p[2]}

    def remote(src, dst, ss, rs, dev):
        return pltpu.make_async_remote_copy(
            src_ref=src,
            dst_ref=dst,
            send_sem=ss,
            recv_sem=rs,
            device_id=dev,
            device_id_type=pl.DeviceIdType.MESH,
        )

    barrier = pltpu.get_barrier_semaphore()
    for off in offsets:
        pl.semaphore_signal(
            barrier, inc=1, device_id=ids(peer(off)), device_id_type=pl.DeviceIdType.MESH
        )

    local = [
        pltpu.make_async_copy(tok_in, rawt, loc_sem.at[2]),
        pltpu.make_async_copy(w1, w1v, loc_sem.at[1]),
        pltpu.make_async_copy(cot_in, rawc, loc_sem.at[3]),
        pltpu.make_async_copy(wo1, woF.at[m], loc_sem.at[4]),
        pltpu.make_async_copy(w2, w2F.at[m], loc_sem.at[5]),
        pltpu.make_async_copy(wo2, wsF.at[m], loc_sem.at[6]),
    ]
    for copy in local:
        copy.start()

    def by_token(raw, rows_of):
        x = jnp.transpose(raw[...], (1, 0, 2))
        for b in range(NC):
            for c in range(2):
                first = (2 * b + c) * RW
                rows_of[:, c, b * RW : (b + 1) * RW] = x[:, first : first + RW]

    local[0].wait()
    by_token(rawt, tok)
    tokT[0] = tok[hr]
    tokS[cl] = tok[:, m, pl.ds(cl * RW, RW)]
    pl.semaphore_wait(barrier, len(offsets))

    zc = {}
    for a in range(1, NH):
        d = lax.rem(hr + a, NH)
        zc[a] = remote(
            tok.at[d, m], tokT.at[a, m], z_send.at[a], z_recv.at[a], ids((d, cl, m))
        )
        zc[a].start()
    xc = []

    def to_spatial(which, src, dst):
        for b in range(1, NC):
            dc = lax.rem(cl + b, NC)
            copy = remote(
                src.at[:, m, pl.ds(dc * RW, RW), :],
                dst.at[cl],
                x_send.at[which, b],
                x_recv.at[which, b],
                ids((hr, dc, m)),
            )
            copy.start()
            xc.append(copy)

    to_spatial(0, tok, tokS)
    wc = []
    for which, (src, dst) in enumerate(((wo1, woF), (w2, w2F), (wo2, wsF))):
        copy = remote(src, dst.at[m], w_send.at[which], w_recv.at[which], ids((hr, cl, sib)))
        copy.start()
        wc.append(copy)

    def head_norm(pT, heads):
        n = pT.shape[-1]
        p3 = pT.reshape(heads, HS, n)
        r = lax.rsqrt(jnp.mean(p3 * p3, axis=1, keepdims=True) + EPS_HEAD)
        return p3 * r, r

    def row_norm(x):
        r = lax.rsqrt(jnp.mean(x * x, axis=-1, keepdims=True) + EPS_ROW)
        return x * r, r

    local[2].wait()
    by_token(rawc, cot)
    cotS[cl] = cot[:, m, pl.ds(cl * RW, RW)]
    to_spatial(1, cot, cotS)
    local[1].wait()
    fc = {}

    hours = jnp.concatenate(
        [hour_row[pl.ds(lax.rem(hr + NH - a, NH), 1), :] for a in range(NH)], axis=1
    ).astype(jnp.float32)
    place = lax.broadcasted_iota(jnp.int32, (1, NT1), 1) % BLK // RW
    hours = jnp.where(
        place == 1,
        pltpu.roll(hours, NT1 - RW, 1),
        jnp.where(place == 2, pltpu.roll(hours, RW, 1), hours),
    )
    hours = jnp.broadcast_to(hours, (128, NT1)).T
    hours_j = hours[:, :1]
    hours = hours.reshape(NT1 // RW, U, RU, 128)
    hours_i = [hours[:, u].reshape(QU, 128).T[:1] for u in range(U)]
    factor = SCORE_SCALE * LOG2E

    def forward(a):
        zc[a].wait_recv()
        half = tokT.at[a, m]
        fc[a] = remote(half, half, f_send.at[a], f_recv.at[a], ids((hr, cl, sib)))
        fc[a].start()

    for a in range(NH):
        if a == 1:
            forward(1)
        if 0 < a < NH - 1:
            forward(a + 1)
        if a > 0:
            fc[a].wait_recv()
        x = tokT[a].reshape(BLK, D).astype(jnp.float32)
        n, _ = row_norm(x)
        n = low(n)
        nrm[a] = n.reshape(2 * NC, U, RU, D)
        cols = slice(a * BLK, (a + 1) * BLK)
        k, rk = head_norm(dot(n, w1v[1]).T, HL)
        kT1[:, :, cols] = k
        kTb1[:, :, cols] = low(k)
        r1k[:, :, cols] = rk
        kn = low(k).reshape(W, BLK).T
        v = low(dot(n, w1v[2]))
        vTb1[:, :, cols] = v.T.reshape(HL, HS, BLK)
        for h in range(HL):
            kb1[h, cols, :] = kn[:, h * HS : (h + 1) * HS]
            vb1[h, cols, :] = v[:, h * HS : (h + 1) * HS]
        if a % 2:
            pair = slice((a // 2) * BLK, (a // 2 + 1) * BLK)
            for u in range(U):
                rows = nrm[a - 1 : a + 1, :, u].reshape(BLK, D)
                q, rq = head_norm(dot(rows, w1v[0]).T, HL)
                qT1[u, :, :, pair] = q
                qTb1[u, :, :, pair] = low(q)
                r1q[u, :, :, pair] = rq

    oc = []
    for u in range(U):
        for h in range(HL):
            e = jnp.where(
                hours_j <= hours_i[u], jnp.exp2(dot(kb1[h], qTb1[u, h]) * factor), 0.0
            )
            li = 1.0 / jnp.sum(e, axis=0, keepdims=True)
            li1[u, h] = li
            eb = low(e)
            E1[u, h] = eb
            oT1[u, h] = dot(vTb1[h], eb) * li
        o1buf[u] = low(oT1[u]).reshape(W, QU).T.reshape(NH, 2, NC, RU, W)
        oc.append([])
        for t, off in enumerate(offsets):
            p = peer(off)
            copy = remote(
                o1buf.at[u, (NH - off[0]) % NH, p[2], p[1]],
                o1S.at[u, m, cl * NH + hr],
                o_send.at[u, t],
                o_recv.at[u, t],
                ids(p),
            )
            copy.start()
            oc[u].append(copy)
        o1S.at[u][m, cl * NH + hr] = o1buf[u, 0, m, cl]

    for copy in local[3:]:
        copy.wait()
    for copy in xc:
        copy.wait_recv()
    for copy in wc:
        copy.wait_recv()
    for u in range(U):
        cot2 = cotS[:, :, u * RU : (u + 1) * RU].reshape(N2, D)
        for half in range(2):
            gT2[u, half * HL : (half + 1) * HL] = low(dot_nt(wsF[half], cot2)).reshape(HL, HS, N2)
    rows = lax.broadcasted_iota(jnp.int32, (N2, N2), 0)
    columns = lax.broadcasted_iota(jnp.int32, (N2, N2), 1)
    per_block = SBLK * RU
    block_j = rows // per_block
    block_i = columns // per_block
    near = rows < 0
    for b in range(NSB):
        for c in range(adj.shape[0]):
            near = near | ((block_i == b) & (block_j == adj[c, b]))
    near = near & (rows % RU == columns % RU)
    near = near.astype(jnp.float32)

    def head_back(nT, r, dT):
        return r * (dT - nT * jnp.mean(nT * dT, axis=1, keepdims=True))

    def merged(ref, first):
        return jnp.concatenate([ref[first + h] for h in range(HL)], axis=-1)

    gc, dc_copies = [[] for u in range(U)], []
    for u in range(U):
        span = pl.ds(u * RU, RU)
        for copy in oc[u]:
            copy.wait_recv()
        hid = tokS[:, :, u * RU : (u + 1) * RU].reshape(N2, D).astype(jnp.float32)
        for half in range(2):
            hid = hid + dot(o1S[u, half].reshape(N2, W), woF[half])
        hid = low(hid).astype(jnp.float32)
        n2f, r2 = row_norm(hid)
        n2 = low(n2f)
        for half in range(2):
            hs = slice(half * HL, (half + 1) * HL)
            q, rq = head_norm(dot(n2, w2F[half, 0]).T, HL)
            qT2[hs] = q
            qTb2[hs] = low(q)
            r2T[0, hs] = rq
            k, rk = head_norm(dot(n2, w2F[half, 1]).T, HL)
            kT2[hs] = k
            kTb2[hs] = low(k)
            r2T[1, hs] = rk
            kn = low(k.reshape(W, N2).T)
            v = low(dot(n2, w2F[half, 2]))
            for h in range(HL):
                kb2[half * HL + h] = kn[:, h * HS : (h + 1) * HS]
                vb2[half * HL + h] = v[:, h * HS : (h + 1) * HS]

        for h in range(2 * HL):
            s = dot(kb2[h], qTb2[h])
            e = near * jnp.exp2(s * factor)
            li = 1.0 / jnp.sum(e, axis=0, keepdims=True)
            p = e * li
            g = gT2[u, h]
            dp = dot(vb2[h], g)
            dl = jnp.sum(p * dp, axis=0, keepdims=True)
            ds = low(p * (dp - dl) * SCORE_SCALE)
            dqT2[h] = dot(kTb2[h], ds)
            dk2[h] = dot_nt(ds, qTb2[h])
            dv2[h] = low(dot_nt(low(p), g))

        dn2 = None
        for half in range(2):
            hs = slice(half * HL, (half + 1) * HL)
            dq = low(head_back(qT2[hs], r2T[0, hs], dqT2[hs]).reshape(W, N2).T)
            dkT = merged(dk2, half * HL).T.reshape(HL, HS, N2)
            dk = low(head_back(kT2[hs], r2T[1, hs], dkT).reshape(W, N2).T)
            dv = merged(dv2, half * HL)
            for c, grad in enumerate((dq, dk, dv)):
                part = dot_nt(grad, w2F[half, c])
                dn2 = part if dn2 is None else dn2 + part
        dh = cotS[:, :, u * RU : (u + 1) * RU].reshape(N2, D).astype(jnp.float32) + r2 * (
            dn2 - n2f * jnp.mean(n2f * dn2, axis=-1, keepdims=True)
        )
        dhb = low(dh)
        for half in range(2):
            g1buf[u, half] = low(dot_nt(dhb, woF[half])).reshape(NS, RU, W)

        for t, off in enumerate(offsets):
            p = peer(off)
            copy = remote(
                g1buf.at[u, p[2], p[1] * NH + p[0]],
                g1T.at[u, off[0], m, cl],
                g_send.at[u, t],
                g_recv.at[u, t],
                ids(p),
            )
            copy.start()
            gc[u].append(copy)
        g1T[u, 0, m, cl] = g1buf.at[u][m, cl * NH + hr]
        dhs[:, :, u * RU : (u + 1) * RU] = dhb.reshape(NC, NH, RU, D)
        for b in range(1, NC):
            dc = lax.rem(cl + b, NC)
            copy = remote(
                dhs.at[dc, :, span],
                dhO.at[cl, :, span],
                d_send.at[u, b],
                d_recv.at[u, b],
                ids((hr, dc, m)),
            )
            copy.start()
            dc_copies.append(copy)
    dhO[cl] = dhs[cl]
    for u in range(U):
        for copy in gc[u]:
            copy.wait_recv()
        gT = g1T[u].reshape(QU, W).T.reshape(HL, HS, QU).astype(jnp.float32)
        for h in range(HL):
            gs = gT[h] * (SCORE_SCALE * li1[u, h])
            dl = jnp.sum(oT1[u, h] * gs, axis=0, keepdims=True)
            gs = low(gs)
            eb = E1[u, h]
            ds = low(eb.astype(jnp.float32) * (dot(vb1[h], gs) - dl))
            dqT1[u, h] = dot(kTb1[h], ds)
            dk = dot_nt(ds, qTb1[u, h])
            dv = dot_nt(eb, gs)
            dk1[h] = dk if u == 0 else dk1[h] + dk
            dv1[h] = dv if u == 0 else dv1[h] + dv
        dq = low(head_back(qT1[u], r1q[u], dqT1[u])).reshape(W, QU).T
        g3.at[0][:, :, :, u] = dq.reshape(NH, 2, NC, RU, W)
    dkT = merged(dk1, 0).T.reshape(HL, HS, NT1)
    dk = low(head_back(kT1[...], r1k[...], dkT)).reshape(W, NT1).T
    dv = low(merged(dv1, 0) * (1.0 / SCORE_SCALE))
    g3[1] = dk.reshape(NH, 2, NC, U, RU, W)
    g3[2] = dv.reshape(NH, 2, NC, U, RU, W)

    def partial(which):
        total = None
        for c in range(3):
            part = dot_nt(g3.at[c][:, which].reshape(NH * HB, W), w1v[c])
            total = part if total is None else total + part
        return total

    psend[...] = low(partial(sib)).reshape(NH, HB, D)
    pc = {}
    for a in (*range(1, NH), 0):
        pc[a] = remote(
            psend.at[a], precv.at[a], p_send.at[a], p_recv.at[a], ids((hr, cl, sib))
        )
        pc[a].start()
    pown[...] = partial(m).reshape(NH, HB, D)

    tc = {}
    for a in (*range(1, NH), 0):
        d = lax.rem(hr + NH - a, NH)
        pc[a].wait_recv()
        dn1 = pown[a] + precv[a].astype(jnp.float32)
        n1f, r1 = row_norm(tokT[a, m].astype(jnp.float32))
        t1 = low(r1 * (dn1 - n1f * jnp.mean(n1f * dn1, axis=-1, keepdims=True)))
        if a > 0:
            t1s[a] = t1
            tc[a] = remote(t1s.at[a], t1O.at[hr], t_send.at[a], t_recv.at[a], ids((d, cl, m)))
            tc[a].start()
        else:
            t1O[hr] = t1
    for copy in dc_copies:
        copy.wait_recv()
    for a in range(1, NH):
        tc[a].wait_recv()
    ec, lc = [], []
    for b in range(NC):
        mine = t1O[:, b * RW : (b + 1) * RW].astype(jnp.float32) + dhO[b].astype(jnp.float32)
        outb[b] = jnp.transpose(low(mine), (1, 0, 2))
        place = pl.ds((2 * b + m) * RW, RW)
        copy = remote(
            outb.at[b], out.at[place], e_send.at[b], e_recv.at[b], ids((hr, cl, sib))
        )
        copy.start()
        ec.append(copy)
        copy = pltpu.make_async_copy(outb.at[b], out.at[place], loc_sem.at[7 + b])
        copy.start()
        lc.append(copy)

    for copy in ec:
        copy.wait()
    for copy in lc:
        copy.wait()
    for copy in (
        list(zc.values()) + list(fc.values()) + xc + wc + sum(oc, []) + sum(gc, []) + dc_copies
        + list(pc.values()) + list(tc.values())
    ):
        copy.wait_send()


def fast_shards(
    mesh,
    tokens,
    cotangent,
    hour_of,
    adjacency,
    temporal_query_key_value,
    time_out,
    spatial_query_key_value,
    space_out,
):
    NH, NC = mesh.shape["hour"], mesh.shape["cluster"]
    rows, SL, D = tokens.shape
    W = time_out.shape[0]
    RW = rows // (2 * NC)
    HB = NC * RW
    NT1 = NH * rows
    NS = NC * NH
    U = 2
    RU = RW // U
    N2 = NS * RU
    QU = NT1 // U
    HL = W // HS
    NO = 2 * NH * NC - 1

    bf, f32 = jnp.bfloat16, jnp.float32
    V = pltpu.VMEM
    dma = pltpu.SemaphoreType.DMA
    hbm = pl.BlockSpec(memory_space=pl.ANY)
    return pl.pallas_call(
        functools.partial(layer_kernel, (NH, NC, RW, D, W)),
        out_shape=jax.ShapeDtypeStruct((rows, SL, D), bf),
        in_specs=[
            hbm,
            hbm,
            pl.BlockSpec(memory_space=pltpu.VMEM),
            pl.BlockSpec(memory_space=pltpu.SMEM),
            hbm,
            hbm,
            hbm,
            hbm,
        ],
        out_specs=hbm,
        scratch_shapes=[
            V((rows, SL, D), bf),
            V((rows, SL, D), bf),
            V((SL, 2, HB, D), bf),
            V((SL, 2, HB, D), bf),
            V((NH, 2, HB, D), bf),
            V((NC, NH, RW, D), bf),
            V((NC, NH, RW, D), bf),
            V((3, D, W), bf),
            V((2, W, D), bf),
            V((2, 3, D, W), bf),
            V((2, W, D), bf),
            V((NH, 2 * NC, U, RU, D), bf),
            V((U, HL, HS, QU), f32),
            V((HL, HS, NT1), f32),
            V((U, HL, 1, QU), f32),
            V((HL, 1, NT1), f32),
            V((U, HL, HS, QU), bf),
            V((HL, NT1, HS), bf),
            V((HL, HS, NT1), bf),
            V((HL, NT1, HS), bf),
            V((HL, HS, NT1), bf),
            V((U, HL, NT1, QU), bf),
            V((U, HL, 1, QU), f32),
            V((U, HL, HS, QU), f32),
            V((U, HL, HS, QU), f32),
            V((HL, NT1, HS), f32),
            V((HL, NT1, HS), f32),
            V((U, NH, 2, NC, RU, W), bf),
            V((U, 2, NS, RU, W), bf),
            V((2 * HL, HS, N2), f32),
            V((2 * HL, HS, N2), f32),
            V((2, 2 * HL, 1, N2), f32),
            V((2 * HL, HS, N2), bf),
            V((2 * HL, N2, HS), bf),
            V((2 * HL, HS, N2), bf),
            V((2 * HL, N2, HS), bf),
            V((U, 2 * HL, HS, N2), bf),
            V((2 * HL, HS, N2), f32),
            V((2 * HL, N2, HS), f32),
            V((2 * HL, N2, HS), bf),
            V((U, 2, NS, RU, W), bf),
            V((U, NH, 2, NC, RU, W), bf),
            V((NC, NH, RW, D), bf),
            V((NC, NH, RW, D), bf),
            V((NH, HB, D), bf),
            V((NH, HB, D), bf),
            V((NH, HB, D), f32),
            V((3, NH, 2, NC, U, RU, W), bf),
            V((NH, HB, D), bf),
            V((NH, HB, D), bf),
            V((NC, RW, SL, D), bf),
            dma((7 + NC,)),
            dma((NH,)),
            dma((NH,)),
            dma((NH,)),
            dma((NH,)),
            dma((2, NC)),
            dma((2, NC)),
            dma((3,)),
            dma((3,)),
            dma((U, NO)),
            dma((U, NO)),
            dma((U, NO)),
            dma((U, NO)),
            dma((U, NC)),
            dma((U, NC)),
            dma((NH,)),
            dma((NH,)),
            dma((NH,)),
            dma((NH,)),
            dma((NC,)),
            dma((NC,)),
        ],
        compiler_params=pltpu.CompilerParams(
            collective_id=0, has_side_effects=True, vmem_limit_bytes=58 << 20
        ),
        name="layer",
    )(
        tokens,
        cotangent,
        hour_of.reshape(NH, rows),
        adjacency.T,
        temporal_query_key_value,
        time_out,
        spatial_query_key_value,
        space_out,
    )


def fits(mesh, tokens):
    NH, NC = mesh.shape["hour"], mesh.shape["cluster"]
    SL = tokens.shape[1] // NC
    rows = tokens.shape[0] // (mesh.shape["group"] * NH)
    return (
        mesh.shape["mp"] == 2
        and SL == NH
        and NC == 2
        and NC * NH == S
        and rows % 128 == 0
        and (rows // (2 * NC)) % 32 == 0
        and NH * rows <= 512
    )


def solution(mesh):
    def run(*args):
        body = functools.partial(fast_shards, mesh) if fits(mesh, args[0]) else shards
        return jax.shard_map(
            body,
            mesh=mesh,
            in_specs=(
                P(("group", "hour"), "cluster", None),
                P(("group", "hour"), "cluster", None),
                P("group"),
                P(),
                P(None, None, "mp"),
                P("mp", None),
                P(None, None, "mp"),
                P("mp", None),
            ),
            out_specs=P(("group", "hour"), "cluster", None),
            check_vma=False,
        )(*args)

    return run
```

```python
import functools

import jax
import jax.numpy as jnp
from jax import lax
from jax.experimental import pallas as pl
from jax.experimental.pallas import tpu as pltpu
from jax.sharding import PartitionSpec as P

HS = 64
SBLK = 2
NSB = 4
S = 8


EPS_ROW = 1e-05
EPS_HEAD = 1e-06
SCORE_SCALE = 0.25
LOG2E = 1.4426950408889634


def row_scale(values, epsilon):
    return lax.rsqrt(jnp.mean(values * values, axis=-1, keepdims=True) + epsilon)


def norm_back(normed, scale, grad):
    return scale * (grad - normed * jnp.mean(normed * grad, axis=-1, keepdims=True))


def split_heads(values):
    return values.reshape(values.shape[:-1] + (values.shape[-1] // HS, HS))


def merge_heads(values):
    return values.reshape(values.shape[:-2] + (values.shape[-2] * values.shape[-1],))


def head_totals(partial_value):
    return lax.psum(partial_value.astype(jnp.bfloat16), "mp").astype(jnp.float32)


def project_normalised_rows(input_tokens, weights):
    scale = row_scale(input_tokens, EPS_ROW)
    normed = input_tokens * scale
    projected = jnp.einsum(
        "tsd,cdq->ctsq", normed.astype(jnp.bfloat16), weights, preferred_element_type=jnp.float32
    )
    query = split_heads(projected[0])
    query_scale = row_scale(query, EPS_HEAD)
    keyed = split_heads(projected[1])
    key_scale = row_scale(keyed, EPS_HEAD)
    values = split_heads(projected[2]).astype(jnp.bfloat16)
    return (normed, scale, query * query_scale, query_scale, keyed * key_scale, key_scale, values)


def input_gradient_rows(
    normed, scale, norm_q, q_scale, norm_k, k_scale, grad_q, grad_k, grad_v, weights
):
    query_grad = norm_back(norm_q, q_scale, grad_q).astype(jnp.bfloat16)
    key_grad = norm_back(norm_k, k_scale, grad_k).astype(jnp.bfloat16)
    stacked = jnp.stack([merge_heads(query_grad), merge_heads(key_grad), merge_heads(grad_v)])
    partial_value = jnp.einsum(
        "ctsq,cdq->tsd", stacked, weights, preferred_element_type=jnp.float32
    )
    return norm_back(normed, scale, head_totals(partial_value))


def shards(
    tokens,
    cotangent,
    hour_of,
    adjacency,
    temporal_query_key_value,
    time_out,
    spatial_query_key_value,
    space_out,
):
    rows = tokens.shape[0]
    local_hours = lax.dynamic_slice_in_dim(hour_of, lax.axis_index("hour") * rows, rows)
    input_tokens = tokens.astype(jnp.float32)
    (
        temporal_normalised,
        temporal_scale,
        temporal_query,
        temporal_query_scale,
        temporal_key,
        temporal_key_scale,
        temporal_value,
    ) = project_normalised_rows(input_tokens, temporal_query_key_value)
    query_low = temporal_query.astype(jnp.bfloat16)
    key_low = temporal_key.astype(jnp.bfloat16)
    key_all, value_all = (
        lax.all_gather(merge_heads(key_low), "hour", axis=0, tiled=True),
        lax.all_gather(merge_heads(temporal_value), "hour", axis=0, tiled=True),
    )
    key_all = split_heads(key_all)
    value_all = split_heads(value_all)
    visible = hour_of[None, :] <= local_hours[:, None]
    scores = (
        jnp.einsum("ishd,jshd->shij", query_low, key_all, preferred_element_type=jnp.float32)
        * SCORE_SCALE
    )
    weights = jnp.where(visible, jnp.exp(scores), 0.0)
    totals = jnp.sum(weights, axis=-1, keepdims=True)
    probs = weights / totals
    probs_low = probs.astype(jnp.bfloat16)
    attended = jnp.einsum(
        "shij,jshd->ishd", probs_low, value_all, preferred_element_type=jnp.float32
    ).astype(jnp.bfloat16)
    mixed = jnp.einsum(
        "isq,qd->isd", merge_heads(attended), time_out, preferred_element_type=jnp.float32
    )
    hidden_state = lax.optimization_barrier(
        (input_tokens + head_totals(mixed)).astype(jnp.bfloat16)
    ).astype(jnp.float32)
    (
        spatial_normalised,
        spatial_scale,
        spatial_query,
        spatial_query_scale,
        spatial_key,
        spatial_key_scale,
        spatial_value,
    ) = project_normalised_rows(hidden_state, spatial_query_key_value)
    grad_out = jnp.einsum(
        "isd,qd->isq", cotangent, space_out, preferred_element_type=jnp.float32
    ).astype(jnp.bfloat16)
    query_near, key_near, value_near, grad_near = (
        lax.all_to_all(
            merge_heads(spatial_query.astype(jnp.bfloat16)),
            "cluster",
            split_axis=0,
            concat_axis=1,
            tiled=True,
        ),
        lax.all_to_all(
            merge_heads(spatial_key.astype(jnp.bfloat16)),
            "cluster",
            split_axis=0,
            concat_axis=1,
            tiled=True,
        ),
        lax.all_to_all(
            merge_heads(spatial_value), "cluster", split_axis=0, concat_axis=1, tiled=True
        ),
        lax.all_to_all(grad_out, "cluster", split_axis=0, concat_axis=1, tiled=True),
    )
    query_near = split_heads(query_near)
    key_near = split_heads(key_near)
    value_near = split_heads(value_near)
    grad_near = split_heads(grad_near)
    block = jnp.arange(S) // SBLK
    listed = jnp.sum(
        (adjacency[:, :, None] == jnp.arange(NSB)[None, None, :]).astype(jnp.float32), axis=1
    )
    member = (block[:, None] == jnp.arange(NSB)[None, :]).astype(jnp.float32)
    near = jnp.dot(jnp.dot(member, listed), member.T) > 0.5
    scores_two = (
        jnp.einsum("rihd,rjhd->rhij", query_near, key_near, preferred_element_type=jnp.float32)
        * SCORE_SCALE
    )
    weights_two = jnp.where(near, jnp.exp(scores_two), 0.0)
    probs_two = weights_two / jnp.sum(weights_two, axis=-1, keepdims=True)
    dprob_two = jnp.einsum(
        "rihd,rjhd->rhij", grad_near, value_near, preferred_element_type=jnp.float32
    )
    delta_two = jnp.sum(probs_two * dprob_two, axis=-1, keepdims=True)
    dscore_two = (probs_two * (dprob_two - delta_two) * SCORE_SCALE).astype(jnp.bfloat16)
    dquery_near = jnp.einsum(
        "rhij,rjhd->rihd", dscore_two, key_near, preferred_element_type=jnp.float32
    ).astype(jnp.bfloat16)
    dkey_near = jnp.einsum(
        "rhij,rihd->rjhd", dscore_two, query_near, preferred_element_type=jnp.float32
    ).astype(jnp.bfloat16)
    dvalue_near = jnp.einsum(
        "rhij,rihd->rjhd",
        probs_two.astype(jnp.bfloat16),
        grad_near,
        preferred_element_type=jnp.float32,
    ).astype(jnp.bfloat16)
    spatial_query_gradient, spatial_key_gradient, spatial_value_gradient = (
        lax.all_to_all(
            merge_heads(dquery_near), "cluster", split_axis=1, concat_axis=0, tiled=True
        ),
        lax.all_to_all(merge_heads(dkey_near), "cluster", split_axis=1, concat_axis=0, tiled=True),
        lax.all_to_all(
            merge_heads(dvalue_near), "cluster", split_axis=1, concat_axis=0, tiled=True
        ),
    )
    hidden_state_gradient = cotangent.astype(jnp.float32) + input_gradient_rows(
        spatial_normalised,
        spatial_scale,
        spatial_query,
        spatial_query_scale,
        spatial_key,
        spatial_key_scale,
        split_heads(spatial_query_gradient).astype(jnp.float32),
        split_heads(spatial_key_gradient).astype(jnp.float32),
        split_heads(spatial_value_gradient),
        spatial_query_key_value,
    )
    grad_low = hidden_state_gradient.astype(jnp.bfloat16)
    grad_one = split_heads(
        jnp.einsum("isd,qd->isq", grad_low, time_out, preferred_element_type=jnp.float32).astype(
            jnp.bfloat16
        )
    )
    dprob = jnp.einsum("ishd,jshd->shij", grad_one, value_all, preferred_element_type=jnp.float32)
    delta = jnp.sum(probs * dprob, axis=-1, keepdims=True)
    dscore = (probs * (dprob - delta) * SCORE_SCALE).astype(jnp.bfloat16)
    temporal_query_gradient = jnp.einsum(
        "shij,jshd->ishd", dscore, key_all, preferred_element_type=jnp.float32
    )
    key_part = jnp.einsum("shij,ishd->jshd", dscore, query_low, preferred_element_type=jnp.float32)
    value_part = jnp.einsum(
        "shij,ishd->jshd", probs_low, grad_one, preferred_element_type=jnp.float32
    )
    summed = lax.psum_scatter(
        jnp.concatenate([merge_heads(key_part), merge_heads(value_part)], axis=-1).astype(
            jnp.bfloat16
        ),
        "hour",
        scatter_dimension=0,
        tiled=True,
    ).astype(jnp.float32)
    half_width = summed.shape[-1] // 2
    temporal_key_gradient = split_heads(summed[..., :half_width])
    temporal_value_gradient = split_heads(summed[..., half_width:])
    input_gradient_total = input_gradient_rows(
        temporal_normalised,
        temporal_scale,
        temporal_query,
        temporal_query_scale,
        temporal_key,
        temporal_key_scale,
        temporal_query_gradient,
        temporal_key_gradient,
        temporal_value_gradient.astype(jnp.bfloat16),
        temporal_query_key_value,
    )
    return (hidden_state_gradient + input_gradient_total).astype(jnp.bfloat16)


NT = (((1,), (1,)), ((), ()))


def dot(a, b):
    return jnp.dot(a, b, preferred_element_type=jnp.float32)


def dot_nt(a, b):
    return lax.dot_general(a, b, NT, preferred_element_type=jnp.float32)


def low(values):
    return values.astype(jnp.bfloat16)


def layer_kernel(
    cfg,
    tok_in,
    cot_in,
    hour_row,
    adj,
    w1,
    wo1,
    w2,
    wo2,
    out,
    rawt,
    rawc,
    tok,
    cot,
    tokT,
    tokS,
    cotS,
    w1v,
    woF,
    w2F,
    wsF,
    nrm,
    qT1,
    kT1,
    r1q,
    r1k,
    qTb1,
    kb1,
    kTb1,
    vb1,
    vTb1,
    E1,
    li1,
    oT1,
    dqT1,
    dkT1,
    dvT1,
    o1buf,
    o1S,
    qT2,
    kT2,
    r2T,
    qTb2,
    kb2,
    kTb2,
    vb2,
    gT2,
    dqT2,
    dkT2,
    dvT2,
    g1buf,
    g1T,
    dhs,
    dhO,
    psend,
    precv,
    pown,
    g3,
    t1s,
    t1O,
    loc_sem,
    z_send,
    z_recv,
    f_send,
    f_recv,
    x_send,
    x_recv,
    w_send,
    w_recv,
    o_send,
    o_recv,
    g_send,
    g_recv,
    d_send,
    d_recv,
    p_send,
    p_recv,
    t_send,
    t_recv,
    e_send,
    e_recv,
):
    NH, NC, RW, D, W = cfg
    HL = W // HS
    HB = NC * RW
    BLK = 2 * HB
    NT1 = NH * BLK
    NS = NC * NH
    U = 2
    RU = RW // U
    N2 = NS * RU
    QU = NT1 // U
    hr = lax.axis_index("hour")
    cl = lax.axis_index("cluster")
    m = lax.axis_index("mp")
    sib = 1 - m
    offsets = [
        (a % NH, b % NC, c)
        for a in (2, 1, *range(3, NH + 1))
        for b in range(1, NC + 1)
        for c in range(2)
        if (a % NH, b % NC, c) != (0, 0, 0)
    ]

    def peer(off):
        return (lax.rem(hr + off[0], NH), lax.rem(cl + off[1], NC), lax.rem(m + off[2], 2))

    def ids(p):
        return {"hour": p[0], "cluster": p[1], "mp": p[2]}

    def remote(src, dst, ss, rs, dev):
        return pltpu.make_async_remote_copy(
            src_ref=src,
            dst_ref=dst,
            send_sem=ss,
            recv_sem=rs,
            device_id=dev,
            device_id_type=pl.DeviceIdType.MESH,
        )

    barrier = pltpu.get_barrier_semaphore()
    for off in offsets:
        pl.semaphore_signal(
            barrier, inc=1, device_id=ids(peer(off)), device_id_type=pl.DeviceIdType.MESH
        )

    local = [
        pltpu.make_async_copy(tok_in, rawt, loc_sem.at[2]),
        pltpu.make_async_copy(w1, w1v, loc_sem.at[1]),
        pltpu.make_async_copy(cot_in, rawc, loc_sem.at[3]),
        pltpu.make_async_copy(wo1, woF.at[m], loc_sem.at[4]),
        pltpu.make_async_copy(w2, w2F.at[m], loc_sem.at[5]),
        pltpu.make_async_copy(wo2, wsF.at[m], loc_sem.at[6]),
    ]
    for copy in local:
        copy.start()

    def by_token(raw, rows_of):
        x = jnp.transpose(raw[...], (1, 0, 2))
        for b in range(NC):
            for c in range(2):
                first = (2 * b + c) * RW
                rows_of[:, c, b * RW : (b + 1) * RW] = x[:, first : first + RW]

    local[0].wait()
    by_token(rawt, tok)
    tokT[0] = tok[hr]
    tokS[cl] = tok[:, m, pl.ds(cl * RW, RW)]
    pl.semaphore_wait(barrier, len(offsets))

    zc = {}
    for a in range(1, NH):
        d = lax.rem(hr + a, NH)
        zc[a] = remote(
            tok.at[d, m], tokT.at[a, m], z_send.at[a], z_recv.at[a], ids((d, cl, m))
        )
        zc[a].start()
    xc = []

    def to_spatial(which, src, dst):
        for b in range(1, NC):
            dc = lax.rem(cl + b, NC)
            copy = remote(
                src.at[:, m, pl.ds(dc * RW, RW), :],
                dst.at[cl],
                x_send.at[which, b],
                x_recv.at[which, b],
                ids((hr, dc, m)),
            )
            copy.start()
            xc.append(copy)

    to_spatial(0, tok, tokS)
    wc = []
    for which, (src, dst) in enumerate(((wo1, woF), (w2, w2F), (wo2, wsF))):
        copy = remote(src, dst.at[m], w_send.at[which], w_recv.at[which], ids((hr, cl, sib)))
        copy.start()
        wc.append(copy)

    def head_norm(pT, heads):
        n = pT.shape[-1]
        p3 = pT.reshape(heads, HS, n)
        r = lax.rsqrt(jnp.mean(p3 * p3, axis=1, keepdims=True) + EPS_HEAD)
        return p3 * r, r

    def row_norm(x):
        r = lax.rsqrt(jnp.mean(x * x, axis=-1, keepdims=True) + EPS_ROW)
        return x * r, r

    local[2].wait()
    by_token(rawc, cot)
    cotS[cl] = cot[:, m, pl.ds(cl * RW, RW)]
    to_spatial(1, cot, cotS)
    local[1].wait()
    fc = {}

    hours = jnp.concatenate(
        [hour_row[pl.ds(lax.rem(hr + NH - a, NH), 1), :] for a in range(NH)], axis=1
    ).astype(jnp.float32)
    place = lax.broadcasted_iota(jnp.int32, (1, NT1), 1) % BLK // RW
    hours = jnp.where(
        place == 1,
        pltpu.roll(hours, NT1 - RW, 1),
        jnp.where(place == 2, pltpu.roll(hours, RW, 1), hours),
    )
    hours = jnp.broadcast_to(hours, (128, NT1)).T
    hours_j = hours[:, :1]
    hours = hours.reshape(NT1 // RW, U, RU, 128)
    hours_i = [hours[:, u].reshape(QU, 128).T[:1] for u in range(U)]
    factor = SCORE_SCALE * LOG2E

    def forward(a):
        zc[a].wait_recv()
        half = tokT.at[a, m]
        fc[a] = remote(half, half, f_send.at[a], f_recv.at[a], ids((hr, cl, sib)))
        fc[a].start()

    for a in range(NH):
        if a == 1:
            forward(1)
        if 0 < a < NH - 1:
            forward(a + 1)
        if a > 0:
            fc[a].wait_recv()
        x = tokT[a].reshape(BLK, D).astype(jnp.float32)
        n, _ = row_norm(x)
        n = low(n)
        nrm[a] = n.reshape(2 * NC, U, RU, D)
        cols = slice(a * BLK, (a + 1) * BLK)
        k, rk = head_norm(dot(n, w1v[1]).T, HL)
        kT1[:, :, cols] = k
        kTb1[:, :, cols] = low(k)
        r1k[:, :, cols] = rk
        kn = low(k).reshape(W, BLK).T
        v = low(dot(n, w1v[2]))
        vTb1[:, :, cols] = v.T.reshape(HL, HS, BLK)
        for h in range(HL):
            kb1[h, cols, :] = kn[:, h * HS : (h + 1) * HS]
            vb1[h, cols, :] = v[:, h * HS : (h + 1) * HS]
        if a % 2:
            pair = slice((a // 2) * BLK, (a // 2 + 1) * BLK)
            for u in range(U):
                rows = nrm[a - 1 : a + 1, :, u].reshape(BLK, D)
                q, rq = head_norm(dot(rows, w1v[0]).T, HL)
                qT1[u, :, :, pair] = q
                qTb1[u, :, :, pair] = low(q)
                r1q[u, :, :, pair] = rq

    oc = []
    for u in range(U):
        for h in range(HL):
            e = jnp.where(
                hours_j <= hours_i[u], jnp.exp2(dot(kb1[h], qTb1[u, h]) * factor), 0.0
            )
            li = 1.0 / jnp.sum(e, axis=0, keepdims=True)
            li1[u, h] = li
            eb = low(e)
            E1[u, h] = eb
            oT1[u, h] = dot(vTb1[h], eb) * li
        o1buf[u] = low(oT1[u]).reshape(W, QU).T.reshape(NH, 2, NC, RU, W)
        oc.append([])
        for t, off in enumerate(offsets):
            p = peer(off)
            copy = remote(
                o1buf.at[u, (NH - off[0]) % NH, p[2], p[1]],
                o1S.at[u, m, cl * NH + hr],
                o_send.at[u, t],
                o_recv.at[u, t],
                ids(p),
            )
            copy.start()
            oc[u].append(copy)
        o1S.at[u][m, cl * NH + hr] = o1buf[u, 0, m, cl]

    for copy in local[3:]:
        copy.wait()
    for copy in xc:
        copy.wait_recv()
    for copy in wc:
        copy.wait_recv()
    for u in range(U):
        cot2 = cotS[:, :, u * RU : (u + 1) * RU].reshape(N2, D)
        for half in range(2):
            gT2[u, half * HL : (half + 1) * HL] = low(dot_nt(wsF[half], cot2)).reshape(HL, HS, N2)
    rows = lax.broadcasted_iota(jnp.int32, (N2, N2), 0)
    columns = lax.broadcasted_iota(jnp.int32, (N2, N2), 1)
    per_block = SBLK * RU
    block_j = rows // per_block
    block_i = columns // per_block
    near = rows < 0
    for b in range(NSB):
        for c in range(adj.shape[0]):
            near = near | ((block_i == b) & (block_j == adj[c, b]))
    near = near & (rows % RU == columns % RU)
    near = near.astype(jnp.float32)

    def head_back(nT, r, dT):
        return r * (dT - nT * jnp.mean(nT * dT, axis=1, keepdims=True))

    gc, dc_copies = [[] for u in range(U)], []
    for u in range(U):
        span = pl.ds(u * RU, RU)
        for copy in oc[u]:
            copy.wait_recv()
        hid = tokS[:, :, u * RU : (u + 1) * RU].reshape(N2, D).astype(jnp.float32)
        for half in range(2):
            hid = hid + dot(o1S[u, half].reshape(N2, W), woF[half])
        hid = low(hid).astype(jnp.float32)
        n2f, r2 = row_norm(hid)
        n2 = low(n2f)
        for half in range(2):
            hs = slice(half * HL, (half + 1) * HL)
            q, rq = head_norm(dot(n2, w2F[half, 0]).T, HL)
            qT2[hs] = q
            qTb2[hs] = low(q)
            r2T[0, hs] = rq
            k, rk = head_norm(dot(n2, w2F[half, 1]).T, HL)
            kT2[hs] = k
            kTb2[hs] = low(k)
            r2T[1, hs] = rk
            kn = low(k).reshape(W, N2).T
            v = low(dot(n2, w2F[half, 2]))
            for h in range(HL):
                kb2[half * HL + h] = kn[:, h * HS : (h + 1) * HS]
                vb2[half * HL + h] = v[:, h * HS : (h + 1) * HS]

        probs, grads = [], []
        for h in range(2 * HL):
            e = near * jnp.exp2(dot(kb2[h], qTb2[h]) * factor)
            probs.append(e * (1.0 / jnp.sum(e, axis=0, keepdims=True)))
        for h in range(2 * HL):
            p, dp = probs[h], dot(vb2[h], gT2[u, h])
            dl = jnp.sum(p * dp, axis=0, keepdims=True)
            grads.append(low(p * (dp - dl) * SCORE_SCALE))
        for h in range(2 * HL):
            dvT2[h] = low(dot_nt(gT2[u, h], low(probs[h])))
        for h in range(2 * HL):
            dqT2[h] = dot(kTb2[h], grads[h])
            dkT2[h] = dot_nt(qTb2[h], grads[h])

        dn2 = None
        for half in range(2):
            hs = slice(half * HL, (half + 1) * HL)
            dq = low(head_back(qT2[hs], r2T[0, hs], dqT2[hs])).reshape(W, N2).T
            dk = low(head_back(kT2[hs], r2T[1, hs], dkT2[hs])).reshape(W, N2).T
            dv = dvT2[hs].reshape(W, N2).T
            for c, grad in enumerate((dq, dk, dv)):
                part = dot_nt(grad, w2F[half, c])
                dn2 = part if dn2 is None else dn2 + part
        dh = cotS[:, :, u * RU : (u + 1) * RU].reshape(N2, D).astype(jnp.float32) + r2 * (
            dn2 - n2f * jnp.mean(n2f * dn2, axis=-1, keepdims=True)
        )
        dhb = low(dh)
        for half in range(2):
            g1buf[u, half] = low(dot_nt(dhb, woF[half])).reshape(NS, RU, W)

        for t, off in enumerate(offsets):
            p = peer(off)
            copy = remote(
                g1buf.at[u, p[2], p[1] * NH + p[0]],
                g1T.at[u, off[0], m, cl],
                g_send.at[u, t],
                g_recv.at[u, t],
                ids(p),
            )
            copy.start()
            gc[u].append(copy)
        g1T[u, 0, m, cl] = g1buf.at[u][m, cl * NH + hr]
        dhs[:, :, u * RU : (u + 1) * RU] = dhb.reshape(NC, NH, RU, D)

    for u in range(U):
        for copy in gc[u]:
            copy.wait_recv()
        if u == U - 1:
            for b in range(1, NC):
                dc = lax.rem(cl + b, NC)
                copy = remote(
                    dhs.at[dc], dhO.at[cl], d_send.at[b], d_recv.at[b], ids((hr, dc, m))
                )
                copy.start()
                dc_copies.append(copy)
            dhO[cl] = dhs[cl]
        gT = g1T[u].reshape(QU, W).T.reshape(HL, HS, QU).astype(jnp.float32)
        for h in range(HL):
            gs = gT[h] * (SCORE_SCALE * li1[u, h])
            dl = jnp.sum(oT1[u, h] * gs, axis=0, keepdims=True)
            gs = low(gs)
            eb = E1[u, h]
            ds = low(eb.astype(jnp.float32) * (dot(vb1[h], gs) - dl))
            dqT1[u, h] = dot(kTb1[h], ds)
            dk = dot_nt(qTb1[u, h], ds)
            dv = dot_nt(gs, eb)
            dkT1[h] = dk if u == 0 else dkT1[h] + dk
            dvT1[h] = dv if u == 0 else dvT1[h] + dv
        dq = low(head_back(qT1[u], r1q[u], dqT1[u])).reshape(W, QU).T
        g3.at[0][:, :, :, u] = dq.reshape(NH, 2, NC, RU, W)
    dk = low(head_back(kT1[...], r1k[...], dkT1[...])).reshape(W, NT1).T
    dv = low(dvT1[...] * (1.0 / SCORE_SCALE)).reshape(W, NT1).T
    g3[1] = dk.reshape(NH, 2, NC, U, RU, W)
    g3[2] = dv.reshape(NH, 2, NC, U, RU, W)

    def partial(which):
        total = None
        for c in range(3):
            part = dot_nt(g3.at[c][:, which].reshape(NH * HB, W), w1v[c])
            total = part if total is None else total + part
        return total

    psend[...] = low(partial(sib)).reshape(NH, HB, D)
    pc = {}
    for a in range(NH - 1, -1, -1):
        pc[a] = remote(
            psend.at[a], precv.at[a], p_send.at[a], p_recv.at[a], ids((hr, cl, sib))
        )
        pc[a].start()
    pown[...] = partial(m).reshape(NH, HB, D)

    tc = {}
    for a in range(NH - 1, -1, -1):
        d = lax.rem(hr + NH - a, NH)
        pc[a].wait_recv()
        dn1 = pown[a] + precv[a].astype(jnp.float32)
        n1f, r1 = row_norm(tokT[a, m].astype(jnp.float32))
        t1 = low(r1 * (dn1 - n1f * jnp.mean(n1f * dn1, axis=-1, keepdims=True)))
        if a > 0:
            t1s[a] = t1
            tc[a] = remote(t1s.at[a], t1O.at[hr], t_send.at[a], t_recv.at[a], ids((d, cl, m)))
            tc[a].start()
        else:
            t1O[hr] = t1
    for copy in dc_copies:
        copy.wait_recv()
    for a in range(1, NH):
        tc[a].wait_recv()
    ec = []
    for b in range(NC):
        mine = t1O[:, b * RW : (b + 1) * RW].astype(jnp.float32) + dhO[b].astype(jnp.float32)
        place = pl.ds((2 * b + m) * RW, RW)
        out[place] = jnp.transpose(low(mine), (1, 0, 2))
        copy = remote(
            out.at[place], out.at[place], e_send.at[b], e_recv.at[b], ids((hr, cl, sib))
        )
        copy.start()
        ec.append(copy)

    for copy in ec:
        copy.wait()
    for copy in (
        list(zc.values()) + list(fc.values()) + xc + wc + sum(oc, []) + sum(gc, []) + dc_copies
        + list(pc.values()) + list(tc.values())
    ):
        copy.wait_send()


def fast_shards(
    mesh,
    tokens,
    cotangent,
    hour_of,
    adjacency,
    temporal_query_key_value,
    time_out,
    spatial_query_key_value,
    space_out,
):
    NH, NC = mesh.shape["hour"], mesh.shape["cluster"]
    rows, SL, D = tokens.shape
    W = time_out.shape[0]
    RW = rows // (2 * NC)
    HB = NC * RW
    NT1 = NH * rows
    NS = NC * NH
    U = 2
    RU = RW // U
    N2 = NS * RU
    QU = NT1 // U
    HL = W // HS
    NO = 2 * NH * NC - 1

    bf, f32 = jnp.bfloat16, jnp.float32
    V = pltpu.VMEM
    dma = pltpu.SemaphoreType.DMA
    hbm = pl.BlockSpec(memory_space=pl.ANY)
    return pl.pallas_call(
        functools.partial(layer_kernel, (NH, NC, RW, D, W)),
        out_shape=pltpu.VMEM((rows, SL, D), bf),
        in_specs=[
            hbm,
            hbm,
            pl.BlockSpec(memory_space=pltpu.VMEM),
            pl.BlockSpec(memory_space=pltpu.SMEM),
            hbm,
            hbm,
            hbm,
            hbm,
        ],
        out_specs=pl.BlockSpec(memory_space=pltpu.VMEM),
        scratch_shapes=[
            V((rows, SL, D), bf),
            V((rows, SL, D), bf),
            V((SL, 2, HB, D), bf),
            V((SL, 2, HB, D), bf),
            V((NH, 2, HB, D), bf),
            V((NC, NH, RW, D), bf),
            V((NC, NH, RW, D), bf),
            V((3, D, W), bf),
            V((2, W, D), bf),
            V((2, 3, D, W), bf),
            V((2, W, D), bf),
            V((NH, 2 * NC, U, RU, D), bf),
            V((U, HL, HS, QU), f32),
            V((HL, HS, NT1), f32),
            V((U, HL, 1, QU), f32),
            V((HL, 1, NT1), f32),
            V((U, HL, HS, QU), bf),
            V((HL, NT1, HS), bf),
            V((HL, HS, NT1), bf),
            V((HL, NT1, HS), bf),
            V((HL, HS, NT1), bf),
            V((U, HL, NT1, QU), bf),
            V((U, HL, 1, QU), f32),
            V((U, HL, HS, QU), f32),
            V((U, HL, HS, QU), f32),
            V((HL, HS, NT1), f32),
            V((HL, HS, NT1), f32),
            V((U, NH, 2, NC, RU, W), bf),
            V((U, 2, NS, RU, W), bf),
            V((2 * HL, HS, N2), f32),
            V((2 * HL, HS, N2), f32),
            V((2, 2 * HL, 1, N2), f32),
            V((2 * HL, HS, N2), bf),
            V((2 * HL, N2, HS), bf),
            V((2 * HL, HS, N2), bf),
            V((2 * HL, N2, HS), bf),
            V((U, 2 * HL, HS, N2), bf),
            V((2 * HL, HS, N2), f32),
            V((2 * HL, HS, N2), f32),
            V((2 * HL, HS, N2), bf),
            V((U, 2, NS, RU, W), bf),
            V((U, NH, 2, NC, RU, W), bf),
            V((NC, NH, RW, D), bf),
            V((NC, NH, RW, D), bf),
            V((NH, HB, D), bf),
            V((NH, HB, D), bf),
            V((NH, HB, D), f32),
            V((3, NH, 2, NC, U, RU, W), bf),
            V((NH, HB, D), bf),
            V((NH, HB, D), bf),
            dma((7,)),
            dma((NH,)),
            dma((NH,)),
            dma((NH,)),
            dma((NH,)),
            dma((2, NC)),
            dma((2, NC)),
            dma((3,)),
            dma((3,)),
            dma((U, NO)),
            dma((U, NO)),
            dma((U, NO)),
            dma((U, NO)),
            dma((NC,)),
            dma((NC,)),
            dma((NH,)),
            dma((NH,)),
            dma((NH,)),
            dma((NH,)),
            dma((NC,)),
            dma((NC,)),
        ],
        compiler_params=pltpu.CompilerParams(
            collective_id=0, has_side_effects=True, vmem_limit_bytes=58 << 20
        ),
        name="layer",
    )(
        tokens,
        cotangent,
        hour_of.reshape(NH, rows),
        adjacency.T,
        temporal_query_key_value,
        time_out,
        spatial_query_key_value,
        space_out,
    )


def fits(mesh, tokens):
    NH, NC = mesh.shape["hour"], mesh.shape["cluster"]
    SL = tokens.shape[1] // NC
    rows = tokens.shape[0] // (mesh.shape["group"] * NH)
    return (
        mesh.shape["mp"] == 2
        and SL == NH
        and NC == 2
        and NC * NH == S
        and rows % 128 == 0
        and (rows // (2 * NC)) % 32 == 0
        and NH * rows <= 512
    )


def solution(mesh):
    def run(*args):
        body = functools.partial(fast_shards, mesh) if fits(mesh, args[0]) else shards
        return jax.shard_map(
            body,
            mesh=mesh,
            in_specs=(
                P(("group", "hour"), "cluster", None),
                P(("group", "hour"), "cluster", None),
                P("group"),
                P(),
                P(None, None, "mp"),
                P("mp", None),
                P(None, None, "mp"),
                P("mp", None),
            ),
            out_specs=P(("group", "hour"), "cluster", None),
            check_vma=False,
        )(*args)

    return run
```

```python
import functools

import jax
import jax.numpy as jnp
from jax import lax
from jax.experimental import pallas as pl
from jax.experimental.pallas import tpu as pltpu
from jax.sharding import PartitionSpec as P

HS = 64
SBLK = 2
NSB = 4
S = 8


EPS_ROW = 1e-05
EPS_HEAD = 1e-06
SCORE_SCALE = 0.25
LOG2E = 1.4426950408889634


def row_scale(values, epsilon):
    return lax.rsqrt(jnp.mean(values * values, axis=-1, keepdims=True) + epsilon)


def norm_back(normed, scale, grad):
    return scale * (grad - normed * jnp.mean(normed * grad, axis=-1, keepdims=True))


def split_heads(values):
    return values.reshape(values.shape[:-1] + (values.shape[-1] // HS, HS))


def merge_heads(values):
    return values.reshape(values.shape[:-2] + (values.shape[-2] * values.shape[-1],))


def head_totals(partial_value):
    return lax.psum(partial_value.astype(jnp.bfloat16), "mp").astype(jnp.float32)


def project_normalised_rows(input_tokens, weights):
    scale = row_scale(input_tokens, EPS_ROW)
    normed = input_tokens * scale
    projected = jnp.einsum(
        "tsd,cdq->ctsq", normed.astype(jnp.bfloat16), weights, preferred_element_type=jnp.float32
    )
    query = split_heads(projected[0])
    query_scale = row_scale(query, EPS_HEAD)
    keyed = split_heads(projected[1])
    key_scale = row_scale(keyed, EPS_HEAD)
    values = split_heads(projected[2]).astype(jnp.bfloat16)
    return (normed, scale, query * query_scale, query_scale, keyed * key_scale, key_scale, values)


def input_gradient_rows(
    normed, scale, norm_q, q_scale, norm_k, k_scale, grad_q, grad_k, grad_v, weights
):
    query_grad = norm_back(norm_q, q_scale, grad_q).astype(jnp.bfloat16)
    key_grad = norm_back(norm_k, k_scale, grad_k).astype(jnp.bfloat16)
    stacked = jnp.stack([merge_heads(query_grad), merge_heads(key_grad), merge_heads(grad_v)])
    partial_value = jnp.einsum(
        "ctsq,cdq->tsd", stacked, weights, preferred_element_type=jnp.float32
    )
    return norm_back(normed, scale, head_totals(partial_value))


def shards(
    tokens,
    cotangent,
    hour_of,
    adjacency,
    temporal_query_key_value,
    time_out,
    spatial_query_key_value,
    space_out,
):
    rows = tokens.shape[0]
    local_hours = lax.dynamic_slice_in_dim(hour_of, lax.axis_index("hour") * rows, rows)
    input_tokens = tokens.astype(jnp.float32)
    (
        temporal_normalised,
        temporal_scale,
        temporal_query,
        temporal_query_scale,
        temporal_key,
        temporal_key_scale,
        temporal_value,
    ) = project_normalised_rows(input_tokens, temporal_query_key_value)
    query_low = temporal_query.astype(jnp.bfloat16)
    key_low = temporal_key.astype(jnp.bfloat16)
    key_all, value_all = (
        lax.all_gather(merge_heads(key_low), "hour", axis=0, tiled=True),
        lax.all_gather(merge_heads(temporal_value), "hour", axis=0, tiled=True),
    )
    key_all = split_heads(key_all)
    value_all = split_heads(value_all)
    visible = hour_of[None, :] <= local_hours[:, None]
    scores = (
        jnp.einsum("ishd,jshd->shij", query_low, key_all, preferred_element_type=jnp.float32)
        * SCORE_SCALE
    )
    weights = jnp.where(visible, jnp.exp(scores), 0.0)
    totals = jnp.sum(weights, axis=-1, keepdims=True)
    probs = weights / totals
    probs_low = probs.astype(jnp.bfloat16)
    attended = jnp.einsum(
        "shij,jshd->ishd", probs_low, value_all, preferred_element_type=jnp.float32
    ).astype(jnp.bfloat16)
    mixed = jnp.einsum(
        "isq,qd->isd", merge_heads(attended), time_out, preferred_element_type=jnp.float32
    )
    hidden_state = lax.optimization_barrier(
        (input_tokens + head_totals(mixed)).astype(jnp.bfloat16)
    ).astype(jnp.float32)
    (
        spatial_normalised,
        spatial_scale,
        spatial_query,
        spatial_query_scale,
        spatial_key,
        spatial_key_scale,
        spatial_value,
    ) = project_normalised_rows(hidden_state, spatial_query_key_value)
    grad_out = jnp.einsum(
        "isd,qd->isq", cotangent, space_out, preferred_element_type=jnp.float32
    ).astype(jnp.bfloat16)
    query_near, key_near, value_near, grad_near = (
        lax.all_to_all(
            merge_heads(spatial_query.astype(jnp.bfloat16)),
            "cluster",
            split_axis=0,
            concat_axis=1,
            tiled=True,
        ),
        lax.all_to_all(
            merge_heads(spatial_key.astype(jnp.bfloat16)),
            "cluster",
            split_axis=0,
            concat_axis=1,
            tiled=True,
        ),
        lax.all_to_all(
            merge_heads(spatial_value), "cluster", split_axis=0, concat_axis=1, tiled=True
        ),
        lax.all_to_all(grad_out, "cluster", split_axis=0, concat_axis=1, tiled=True),
    )
    query_near = split_heads(query_near)
    key_near = split_heads(key_near)
    value_near = split_heads(value_near)
    grad_near = split_heads(grad_near)
    block = jnp.arange(S) // SBLK
    listed = jnp.sum(
        (adjacency[:, :, None] == jnp.arange(NSB)[None, None, :]).astype(jnp.float32), axis=1
    )
    member = (block[:, None] == jnp.arange(NSB)[None, :]).astype(jnp.float32)
    near = jnp.dot(jnp.dot(member, listed), member.T) > 0.5
    scores_two = (
        jnp.einsum("rihd,rjhd->rhij", query_near, key_near, preferred_element_type=jnp.float32)
        * SCORE_SCALE
    )
    weights_two = jnp.where(near, jnp.exp(scores_two), 0.0)
    probs_two = weights_two / jnp.sum(weights_two, axis=-1, keepdims=True)
    dprob_two = jnp.einsum(
        "rihd,rjhd->rhij", grad_near, value_near, preferred_element_type=jnp.float32
    )
    delta_two = jnp.sum(probs_two * dprob_two, axis=-1, keepdims=True)
    dscore_two = (probs_two * (dprob_two - delta_two) * SCORE_SCALE).astype(jnp.bfloat16)
    dquery_near = jnp.einsum(
        "rhij,rjhd->rihd", dscore_two, key_near, preferred_element_type=jnp.float32
    ).astype(jnp.bfloat16)
    dkey_near = jnp.einsum(
        "rhij,rihd->rjhd", dscore_two, query_near, preferred_element_type=jnp.float32
    ).astype(jnp.bfloat16)
    dvalue_near = jnp.einsum(
        "rhij,rihd->rjhd",
        probs_two.astype(jnp.bfloat16),
        grad_near,
        preferred_element_type=jnp.float32,
    ).astype(jnp.bfloat16)
    spatial_query_gradient, spatial_key_gradient, spatial_value_gradient = (
        lax.all_to_all(
            merge_heads(dquery_near), "cluster", split_axis=1, concat_axis=0, tiled=True
        ),
        lax.all_to_all(merge_heads(dkey_near), "cluster", split_axis=1, concat_axis=0, tiled=True),
        lax.all_to_all(
            merge_heads(dvalue_near), "cluster", split_axis=1, concat_axis=0, tiled=True
        ),
    )
    hidden_state_gradient = cotangent.astype(jnp.float32) + input_gradient_rows(
        spatial_normalised,
        spatial_scale,
        spatial_query,
        spatial_query_scale,
        spatial_key,
        spatial_key_scale,
        split_heads(spatial_query_gradient).astype(jnp.float32),
        split_heads(spatial_key_gradient).astype(jnp.float32),
        split_heads(spatial_value_gradient),
        spatial_query_key_value,
    )
    grad_low = hidden_state_gradient.astype(jnp.bfloat16)
    grad_one = split_heads(
        jnp.einsum("isd,qd->isq", grad_low, time_out, preferred_element_type=jnp.float32).astype(
            jnp.bfloat16
        )
    )
    dprob = jnp.einsum("ishd,jshd->shij", grad_one, value_all, preferred_element_type=jnp.float32)
    delta = jnp.sum(probs * dprob, axis=-1, keepdims=True)
    dscore = (probs * (dprob - delta) * SCORE_SCALE).astype(jnp.bfloat16)
    temporal_query_gradient = jnp.einsum(
        "shij,jshd->ishd", dscore, key_all, preferred_element_type=jnp.float32
    )
    key_part = jnp.einsum("shij,ishd->jshd", dscore, query_low, preferred_element_type=jnp.float32)
    value_part = jnp.einsum(
        "shij,ishd->jshd", probs_low, grad_one, preferred_element_type=jnp.float32
    )
    summed = lax.psum_scatter(
        jnp.concatenate([merge_heads(key_part), merge_heads(value_part)], axis=-1).astype(
            jnp.bfloat16
        ),
        "hour",
        scatter_dimension=0,
        tiled=True,
    ).astype(jnp.float32)
    half_width = summed.shape[-1] // 2
    temporal_key_gradient = split_heads(summed[..., :half_width])
    temporal_value_gradient = split_heads(summed[..., half_width:])
    input_gradient_total = input_gradient_rows(
        temporal_normalised,
        temporal_scale,
        temporal_query,
        temporal_query_scale,
        temporal_key,
        temporal_key_scale,
        temporal_query_gradient,
        temporal_key_gradient,
        temporal_value_gradient.astype(jnp.bfloat16),
        temporal_query_key_value,
    )
    return (hidden_state_gradient + input_gradient_total).astype(jnp.bfloat16)


NT = (((1,), (1,)), ((), ()))


def dot(a, b):
    return jnp.dot(a, b, preferred_element_type=jnp.float32)


def dot_nt(a, b):
    return lax.dot_general(a, b, NT, preferred_element_type=jnp.float32)


def low(values):
    return values.astype(jnp.bfloat16)


def layer_kernel(
    cfg,
    tok_in,
    cot_in,
    hour_row,
    adj,
    w1,
    wo1,
    w2,
    wo2,
    out,
    rawt,
    rawc,
    tok,
    cot,
    tokT,
    tokS,
    cotS,
    w1v,
    w1T,
    w2T,
    woT,
    woF,
    w2F,
    wsF,
    nrm,
    qT1,
    kT1,
    r1q,
    r1k,
    qTb1,
    kb1,
    kTb1,
    vb1,
    vTb1,
    E1,
    li1,
    oT1,
    dqT1,
    dkT1,
    dvT1,
    o1buf,
    o1S,
    qT2,
    kT2,
    r2T,
    qTb2,
    kb2,
    kTb2,
    vb2,
    gT2,
    dqT2,
    dkT2,
    dvT2,
    g1buf,
    g1T,
    dhs,
    dhO,
    psend,
    precv,
    pown,
    g3,
    t1s,
    t1O,
    loc_sem,
    z_send,
    z_recv,
    f_send,
    f_recv,
    x_send,
    x_recv,
    w_send,
    w_recv,
    o_send,
    o_recv,
    g_send,
    g_recv,
    d_send,
    d_recv,
    p_send,
    p_recv,
    t_send,
    t_recv,
    e_send,
    e_recv,
):
    NH, NC, RW, D, W = cfg
    HL = W // HS
    HB = NC * RW
    BLK = 2 * HB
    NT1 = NH * BLK
    NS = NC * NH
    U = 2
    RU = RW // U
    N2 = NS * RU
    QU = NT1 // U
    hr = lax.axis_index("hour")
    cl = lax.axis_index("cluster")
    m = lax.axis_index("mp")
    sib = 1 - m
    offsets = [
        (a % NH, b % NC, c)
        for a in (2, 1, *range(3, NH + 1))
        for b in range(1, NC + 1)
        for c in range(2)
        if (a % NH, b % NC, c) != (0, 0, 0)
    ]

    def peer(off):
        return (lax.rem(hr + off[0], NH), lax.rem(cl + off[1], NC), lax.rem(m + off[2], 2))

    def ids(p):
        return {"hour": p[0], "cluster": p[1], "mp": p[2]}

    def remote(src, dst, ss, rs, dev):
        return pltpu.make_async_remote_copy(
            src_ref=src,
            dst_ref=dst,
            send_sem=ss,
            recv_sem=rs,
            device_id=dev,
            device_id_type=pl.DeviceIdType.MESH,
        )

    barrier = pltpu.get_barrier_semaphore()
    for off in offsets:
        pl.semaphore_signal(
            barrier, inc=1, device_id=ids(peer(off)), device_id_type=pl.DeviceIdType.MESH
        )

    halves = []
    for c, half in enumerate((m, sib)):
        halves.append([])
        for b in range(NC):
            span = pl.ds((2 * b + half) * RW, RW)
            halves[c].append(
                pltpu.make_async_copy(tok_in.at[span], rawt.at[span], loc_sem.at[6 + c * NC + b])
            )
    local = halves[0] + [
        pltpu.make_async_copy(w1, w1v, loc_sem.at[1]),
        pltpu.make_async_copy(cot_in, rawc, loc_sem.at[2]),
        pltpu.make_async_copy(wo1, woF.at[m], loc_sem.at[3]),
        pltpu.make_async_copy(w2, w2F.at[m], loc_sem.at[4]),
        pltpu.make_async_copy(wo2, wsF.at[m], loc_sem.at[5]),
    ]
    local[NC:NC] = halves[1]
    for copy in local:
        copy.start()
    local = [None] + local[2 * NC :]

    def by_token(raw, rows_of):
        x = jnp.transpose(raw[...], (1, 0, 2))
        for b in range(NC):
            for c in range(2):
                first = (2 * b + c) * RW
                rows_of[:, c, b * RW : (b + 1) * RW] = x[:, first : first + RW]

    def half_by_token(c, half):
        for b in range(NC):
            halves[c][b].wait()
            x = jnp.transpose(rawt[pl.ds((2 * b + half) * RW, RW)], (1, 0, 2))
            tok[:, half, b * RW : (b + 1) * RW] = x

    half_by_token(0, m)
    tokS[cl] = tok[:, m, pl.ds(cl * RW, RW)]
    pl.semaphore_wait(barrier, len(offsets))

    zc = {}
    for a in range(1, NH):
        d = lax.rem(hr + a, NH)
        zc[a] = remote(
            tok.at[d, m], tokT.at[a, m], z_send.at[a], z_recv.at[a], ids((d, cl, m))
        )
        zc[a].start()
    xc = []

    def to_spatial(which, src, dst):
        for b in range(1, NC):
            dc = lax.rem(cl + b, NC)
            copy = remote(
                src.at[:, m, pl.ds(dc * RW, RW), :],
                dst.at[cl],
                x_send.at[which, b],
                x_recv.at[which, b],
                ids((hr, dc, m)),
            )
            copy.start()
            xc.append(copy)

    to_spatial(0, tok, tokS)
    half_by_token(1, sib)
    tokT[0] = tok[hr]
    wc = []
    for which, (src, dst) in enumerate(((wo1, woF), (w2, w2F), (wo2, wsF))):
        copy = remote(src, dst.at[m], w_send.at[which], w_recv.at[which], ids((hr, cl, sib)))
        copy.start()
        wc.append(copy)

    def head_norm(pT, heads):
        n = pT.shape[-1]
        p3 = pT.reshape(heads, HS, n)
        r = lax.rsqrt(jnp.mean(p3 * p3, axis=1, keepdims=True) + EPS_HEAD)
        return p3 * r, r

    def row_norm(x):
        r = lax.rsqrt(jnp.mean(x * x, axis=-1, keepdims=True) + EPS_ROW)
        return x * r, r

    local[2].wait()
    by_token(rawc, cot)
    cotS[cl] = cot[:, m, pl.ds(cl * RW, RW)]
    to_spatial(1, cot, cotS)
    local[1].wait()
    local[4].wait()
    for c in range(3):
        w1T[c * W : (c + 1) * W] = w1v[c].T
        w2T[m, c] = w2F[m, c].T
    fc = {}

    hours = jnp.concatenate(
        [hour_row[pl.ds(lax.rem(hr + NH - a, NH), 1), :] for a in range(NH)], axis=1
    ).astype(jnp.float32)
    place = lax.broadcasted_iota(jnp.int32, (1, NT1), 1) % BLK // RW
    hours = jnp.where(
        place == 1,
        pltpu.roll(hours, NT1 - RW, 1),
        jnp.where(place == 2, pltpu.roll(hours, RW, 1), hours),
    )
    hours = jnp.broadcast_to(hours, (128, NT1)).T
    hours_j = hours[:, :1]
    hours = hours.reshape(NT1 // RW, U, RU, 128)
    hours_i = [hours[:, u].reshape(QU, 128).T[:1] for u in range(U)]
    factor = SCORE_SCALE * LOG2E

    def forward(a):
        zc[a].wait_recv()
        half = tokT.at[a, m]
        fc[a] = remote(half, half, f_send.at[a], f_recv.at[a], ids((hr, cl, sib)))
        fc[a].start()

    def project_queries(u, p):
        pair = slice(p * BLK, (p + 1) * BLK)
        rows = nrm[2 * p : 2 * p + 2, :, u].reshape(BLK, D)
        q, rq = head_norm(dot(rows, w1v[0]).T, HL)
        qT1[u, :, :, pair] = q
        qTb1[u, :, :, pair] = low(q)
        r1q[u, :, :, pair] = rq

    for a in range(NH):
        if a == 1:
            forward(1)
        if 0 < a < NH - 1:
            forward(a + 1)
        if a > 0:
            fc[a].wait_recv()
        if a == 1:
            wc[1].wait_recv()
            for c in range(3):
                w2T[sib, c] = w2F[sib, c].T
            local[3].wait()
            wc[0].wait_recv()
            for half in range(2):
                woT[:, half * W : (half + 1) * W] = woF[half].T
        x = tokT[a].reshape(BLK, D).astype(jnp.float32)
        n, _ = row_norm(x)
        n = low(n)
        nrm[a] = n.reshape(2 * NC, U, RU, D)
        cols = slice(a * BLK, (a + 1) * BLK)
        k, rk = head_norm(dot(n, w1v[1]).T, HL)
        kT1[:, :, cols] = k
        kTb1[:, :, cols] = low(k)
        r1k[:, :, cols] = rk
        kn = low(k).reshape(W, BLK).T
        v = low(dot(n, w1v[2]))
        vTb1[:, :, cols] = v.T.reshape(HL, HS, BLK)
        for h in range(HL):
            kb1[h, cols, :] = kn[:, h * HS : (h + 1) * HS]
            vb1[h, cols, :] = v[:, h * HS : (h + 1) * HS]
        if a % 2:
            for u in range(U if a < NH - 1 else 1):
                project_queries(u, a // 2)

    oc = []
    for u in range(U):
        if u > 0:
            project_queries(u, NH // 2 - 1)
        for h in range(HL):
            e = jnp.where(
                hours_j <= hours_i[u], jnp.exp2(dot(kb1[h], qTb1[u, h]) * factor), 0.0
            )
            li1[u, h] = 1.0 / jnp.sum(e, axis=0, keepdims=True)
            E1[u, h] = low(e)
        for h in range(HL):
            oT1[u, h] = dot(vTb1[h], E1[u, h]) * li1[u, h]
        o1buf[u] = low(oT1[u]).reshape(W, QU).T.reshape(NH, 2, NC, RU, W)
        oc.append([])
        for t, off in enumerate(offsets):
            p = peer(off)
            copy = remote(
                o1buf.at[u, (NH - off[0]) % NH, p[2], p[1]],
                o1S.at[u, m, cl * NH + hr],
                o_send.at[u, t],
                o_recv.at[u, t],
                ids(p),
            )
            copy.start()
            oc[u].append(copy)
        o1S.at[u][m, cl * NH + hr] = o1buf[u, 0, m, cl]

    local[5].wait()
    for copy in xc:
        copy.wait_recv()
    wc[2].wait_recv()
    for copy in list(zc.values()) + list(fc.values()) + xc + wc:
        copy.wait_send()
    for u in range(U):
        cot2 = cotS[:, :, u * RU : (u + 1) * RU].reshape(N2, D)
        for half in range(2):
            gT2[u, half * HL : (half + 1) * HL] = low(dot_nt(wsF[half], cot2)).reshape(HL, HS, N2)
    rows = lax.broadcasted_iota(jnp.int32, (N2, N2), 0)
    columns = lax.broadcasted_iota(jnp.int32, (N2, N2), 1)
    per_block = SBLK * RU
    block_j = rows // per_block
    block_i = columns // per_block
    near = rows < 0
    for b in range(NSB):
        for c in range(adj.shape[0]):
            near = near | ((block_i == b) & (block_j == adj[c, b]))
    near = near & (rows % RU == columns % RU)
    near = near.astype(jnp.float32)

    def head_back(nT, r, dT):
        return r * (dT - nT * jnp.mean(nT * dT, axis=1, keepdims=True))

    gc, dc_copies = [[] for u in range(U)], []
    for u in range(U):
        span = pl.ds(u * RU, RU)
        for copy in oc[u]:
            copy.wait_recv()
        hid = tokS[:, :, u * RU : (u + 1) * RU].reshape(N2, D).astype(jnp.float32)
        o1 = jnp.concatenate([o1S[u, half].reshape(N2, W) for half in range(2)], axis=-1)
        hid = hid + dot(o1, woF[...].reshape(2 * W, D))
        hid = low(hid).astype(jnp.float32)
        n2f, r2 = row_norm(hid)
        n2 = low(n2f)
        for half in range(2):
            hs = slice(half * HL, (half + 1) * HL)
            q, rq = head_norm(dot(n2, w2F[half, 0]).T, HL)
            qT2[hs] = q
            qTb2[hs] = low(q)
            r2T[0, hs] = rq
            k, rk = head_norm(dot(n2, w2F[half, 1]).T, HL)
            kT2[hs] = k
            kTb2[hs] = low(k)
            r2T[1, hs] = rk
            kn = low(k).reshape(W, N2).T
            v = low(dot(n2, w2F[half, 2]))
            for h in range(HL):
                kb2[half * HL + h] = kn[:, h * HS : (h + 1) * HS]
                vb2[half * HL + h] = v[:, h * HS : (h + 1) * HS]

        probs, grads = [], []
        for h in range(2 * HL):
            e = near * jnp.exp2(dot(kb2[h], qTb2[h]) * factor)
            probs.append(e * (1.0 / jnp.sum(e, axis=0, keepdims=True)))
        for h in range(2 * HL):
            p, dp = probs[h], dot(vb2[h], gT2[u, h])
            dl = jnp.sum(p * dp, axis=0, keepdims=True)
            grads.append(low(p * (dp - dl) * SCORE_SCALE))
        for h in range(2 * HL):
            dvT2[h] = low(dot_nt(gT2[u, h], low(probs[h])))
        for h in range(2 * HL):
            dqT2[h] = dot(kTb2[h], grads[h])
            dkT2[h] = dot_nt(qTb2[h], grads[h])

        grads = []
        for half in range(2):
            hs = slice(half * HL, (half + 1) * HL)
            dq = low(head_back(qT2[hs], r2T[0, hs], dqT2[hs])).reshape(W, N2).T
            dk = low(head_back(kT2[hs], r2T[1, hs], dkT2[hs])).reshape(W, N2).T
            grads += [dq, dk, dvT2[hs].reshape(W, N2).T]
        dn2 = dot(jnp.concatenate(grads, axis=-1), w2T[...].reshape(6 * W, D))
        dh = cotS[:, :, u * RU : (u + 1) * RU].reshape(N2, D).astype(jnp.float32) + r2 * (
            dn2 - n2f * jnp.mean(n2f * dn2, axis=-1, keepdims=True)
        )
        dhb = low(dh)
        g1 = low(dot(dhb, woT[...]))
        for half in range(2):
            g1buf[u, half] = g1[:, half * W : (half + 1) * W].reshape(NS, RU, W)

        for t, off in enumerate(offsets):
            p = peer(off)
            copy = remote(
                g1buf.at[u, p[2], p[1] * NH + p[0]],
                g1T.at[u, off[0], m, cl],
                g_send.at[u, t],
                g_recv.at[u, t],
                ids(p),
            )
            copy.start()
            gc[u].append(copy)
        g1T[u, 0, m, cl] = g1buf.at[u][m, cl * NH + hr]
        dhs[:, :, u * RU : (u + 1) * RU] = dhb.reshape(NC, NH, RU, D)

    for copy in sum(oc, []):
        copy.wait_send()
    for u in range(U):
        for copy in gc[u]:
            copy.wait_recv()
        if u == U - 1:
            for b in range(1, NC):
                dc = lax.rem(cl + b, NC)
                copy = remote(
                    dhs.at[dc], dhO.at[cl], d_send.at[b], d_recv.at[b], ids((hr, dc, m))
                )
                copy.start()
                dc_copies.append(copy)
            dhO[cl] = dhs[cl]
        gT = g1T[u].reshape(QU, W).T.reshape(HL, HS, QU).astype(jnp.float32)
        gs = gT * (SCORE_SCALE * li1[u])
        dl = jnp.sum(oT1[u] * gs, axis=1, keepdims=True)
        gs = low(gs)
        ds = []
        for h in range(HL):
            dp = dot(vb1[h], gs[h])
            ds.append(low(E1[u, h].astype(jnp.float32) * (dp - dl[h])))
        for h in range(HL):
            dv = dot_nt(gs[h], E1[u, h])
            dvT1[h] = dv if u == 0 else dvT1[h] + dv
        for h in range(HL):
            dqT1[u, h] = dot(kTb1[h], ds[h])
            dk = dot_nt(qTb1[u, h], ds[h])
            dkT1[h] = dk if u == 0 else dkT1[h] + dk
        dq = low(head_back(qT1[u], r1q[u], dqT1[u])).reshape(W, QU).T
        g3[:, :, :, u, :, :W] = dq.reshape(NH, 2, NC, RU, W)
    dk = low(head_back(kT1[...], r1k[...], dkT1[...])).reshape(W, NT1).T
    dv = low(dvT1[...] * (1.0 / SCORE_SCALE)).reshape(W, NT1).T
    g3[..., W : 2 * W] = dk.reshape(NH, 2, NC, U, RU, W)
    g3[..., 2 * W :] = dv.reshape(NH, 2, NC, U, RU, W)

    def partial(which, span):
        rows = g3[span, which].reshape(-1, 3 * W)
        return dot(rows, w1T[...]).reshape(-1, HB, D)

    pc, tc = {}, {}
    spans = [slice(first, first + 2) for first in range(NH - 2, -1, -2)]
    for span in spans:
        psend[span] = low(partial(sib, span))
        for a in range(span.stop - 1, span.start - 1, -1):
            pc[a] = remote(
                psend.at[a], precv.at[a], p_send.at[a], p_recv.at[a], ids((hr, cl, sib))
            )
            pc[a].start()
    for span in spans:
        pown[span] = partial(m, span)
        for a in range(span.stop - 1, span.start - 1, -1):
            pc[a].wait_recv()
            dn1 = pown[a] + precv[a].astype(jnp.float32)
            n1f, r1 = row_norm(tokT[a, m].astype(jnp.float32))
            t1 = low(r1 * (dn1 - n1f * jnp.mean(n1f * dn1, axis=-1, keepdims=True)))
            if a == 0:
                t1O[hr] = t1
                continue
            t1s[a] = t1
            d = lax.rem(hr + NH - a, NH)
            for b in range(NC):
                rows = pl.ds(b * RW, RW)
                tc[a, b] = remote(
                    t1s.at[a, rows],
                    t1O.at[hr, rows],
                    t_send.at[a, b],
                    t_recv.at[a, b],
                    ids((d, cl, m)),
                )
                tc[a, b].start()
    for copy in dc_copies:
        copy.wait_recv()
    for copy in sum(gc, []) + dc_copies + list(pc.values()):
        copy.wait_send()
    ec = []
    for b in range(NC):
        for a in range(NH - 1, 0, -1):
            tc[a, b].wait_recv()
        mine = t1O[:, b * RW : (b + 1) * RW].astype(jnp.float32) + dhO[b].astype(jnp.float32)
        place = pl.ds((2 * b + m) * RW, RW)
        out[place] = jnp.transpose(low(mine), (1, 0, 2))
        copy = remote(
            out.at[place], out.at[place], e_send.at[b], e_recv.at[b], ids((hr, cl, sib))
        )
        copy.start()
        ec.append(copy)

    for copy in tc.values():
        copy.wait_send()
    for copy in ec:
        copy.wait()


def fast_shards(
    mesh,
    tokens,
    cotangent,
    hour_of,
    adjacency,
    temporal_query_key_value,
    time_out,
    spatial_query_key_value,
    space_out,
):
    NH, NC = mesh.shape["hour"], mesh.shape["cluster"]
    rows, SL, D = tokens.shape
    W = time_out.shape[0]
    RW = rows // (2 * NC)
    HB = NC * RW
    NT1 = NH * rows
    NS = NC * NH
    U = 2
    RU = RW // U
    N2 = NS * RU
    QU = NT1 // U
    HL = W // HS
    NO = 2 * NH * NC - 1

    bf, f32 = jnp.bfloat16, jnp.float32
    V = pltpu.VMEM
    dma = pltpu.SemaphoreType.DMA
    hbm = pl.BlockSpec(memory_space=pl.ANY)
    return pl.pallas_call(
        functools.partial(layer_kernel, (NH, NC, RW, D, W)),
        out_shape=pltpu.VMEM((rows, SL, D), bf),
        in_specs=[
            hbm,
            hbm,
            pl.BlockSpec(memory_space=pltpu.VMEM),
            pl.BlockSpec(memory_space=pltpu.SMEM),
            hbm,
            hbm,
            hbm,
            hbm,
        ],
        out_specs=pl.BlockSpec(memory_space=pltpu.VMEM),
        scratch_shapes=[
            V((rows, SL, D), bf),
            V((rows, SL, D), bf),
            V((SL, 2, HB, D), bf),
            V((SL, 2, HB, D), bf),
            V((NH, 2, HB, D), bf),
            V((NC, NH, RW, D), bf),
            V((NC, NH, RW, D), bf),
            V((3, D, W), bf),
            V((3 * W, D), bf),
            V((2, 3, W, D), bf),
            V((D, 2 * W), bf),
            V((2, W, D), bf),
            V((2, 3, D, W), bf),
            V((2, W, D), bf),
            V((NH, 2 * NC, U, RU, D), bf),
            V((U, HL, HS, QU), f32),
            V((HL, HS, NT1), f32),
            V((U, HL, 1, QU), f32),
            V((HL, 1, NT1), f32),
            V((U, HL, HS, QU), bf),
            V((HL, NT1, HS), bf),
            V((HL, HS, NT1), bf),
            V((HL, NT1, HS), bf),
            V((HL, HS, NT1), bf),
            V((U, HL, NT1, QU), bf),
            V((U, HL, 1, QU), f32),
            V((U, HL, HS, QU), f32),
            V((U, HL, HS, QU), f32),
            V((HL, HS, NT1), f32),
            V((HL, HS, NT1), f32),
            V((U, NH, 2, NC, RU, W), bf),
            V((U, 2, NS, RU, W), bf),
            V((2 * HL, HS, N2), f32),
            V((2 * HL, HS, N2), f32),
            V((2, 2 * HL, 1, N2), f32),
            V((2 * HL, HS, N2), bf),
            V((2 * HL, N2, HS), bf),
            V((2 * HL, HS, N2), bf),
            V((2 * HL, N2, HS), bf),
            V((U, 2 * HL, HS, N2), bf),
            V((2 * HL, HS, N2), f32),
            V((2 * HL, HS, N2), f32),
            V((2 * HL, HS, N2), bf),
            V((U, 2, NS, RU, W), bf),
            V((U, NH, 2, NC, RU, W), bf),
            V((NC, NH, RW, D), bf),
            V((NC, NH, RW, D), bf),
            V((NH, HB, D), bf),
            V((NH, HB, D), bf),
            V((NH, HB, D), f32),
            V((NH, 2, NC, U, RU, 3 * W), bf),
            V((NH, HB, D), bf),
            V((NH, HB, D), bf),
            dma((6 + 2 * NC,)),
            dma((NH,)),
            dma((NH,)),
            dma((NH,)),
            dma((NH,)),
            dma((2, NC)),
            dma((2, NC)),
            dma((3,)),
            dma((3,)),
            dma((U, NO)),
            dma((U, NO)),
            dma((U, NO)),
            dma((U, NO)),
            dma((NC,)),
            dma((NC,)),
            dma((NH,)),
            dma((NH,)),
            dma((NH, NC)),
            dma((NH, NC)),
            dma((NC,)),
            dma((NC,)),
        ],
        compiler_params=pltpu.CompilerParams(
            collective_id=0, has_side_effects=True, vmem_limit_bytes=58 << 20
        ),
        name="layer",
    )(
        tokens,
        cotangent,
        hour_of.reshape(NH, rows),
        adjacency.T,
        temporal_query_key_value,
        time_out,
        spatial_query_key_value,
        space_out,
    )


def fits(mesh, tokens):
    NH, NC = mesh.shape["hour"], mesh.shape["cluster"]
    SL = tokens.shape[1] // NC
    rows = tokens.shape[0] // (mesh.shape["group"] * NH)
    return (
        mesh.shape["mp"] == 2
        and SL == NH
        and NC == 2
        and NC * NH == S
        and rows % 128 == 0
        and (rows // (2 * NC)) % 32 == 0
        and NH * rows <= 512
    )


def solution(mesh):
    def run(*args):
        body = functools.partial(fast_shards, mesh) if fits(mesh, args[0]) else shards
        return jax.shard_map(
            body,
            mesh=mesh,
            in_specs=(
                P(("group", "hour"), "cluster", None),
                P(("group", "hour"), "cluster", None),
                P("group"),
                P(),
                P(None, None, "mp"),
                P("mp", None),
                P(None, None, "mp"),
                P("mp", None),
            ),
            out_specs=P(("group", "hour"), "cluster", None),
            check_vma=False,
        )(*args)

    return run
```

```python
import functools

import jax
import jax.numpy as jnp
from jax import lax
from jax.experimental import pallas as pl
from jax.experimental.pallas import tpu as pltpu
from jax.sharding import PartitionSpec as P

HS = 64
SBLK = 2
NSB = 4
S = 8


EPS_ROW = 1e-05
EPS_HEAD = 1e-06
SCORE_SCALE = 0.25
LOG2E = 1.4426950408889634


def row_scale(values, epsilon):
    return lax.rsqrt(jnp.mean(values * values, axis=-1, keepdims=True) + epsilon)


def norm_back(normed, scale, grad):
    return scale * (grad - normed * jnp.mean(normed * grad, axis=-1, keepdims=True))


def split_heads(values):
    return values.reshape(values.shape[:-1] + (values.shape[-1] // HS, HS))


def merge_heads(values):
    return values.reshape(values.shape[:-2] + (values.shape[-2] * values.shape[-1],))


def head_totals(partial_value):
    return lax.psum(partial_value.astype(jnp.bfloat16), "mp").astype(jnp.float32)


def project_normalised_rows(input_tokens, weights):
    scale = row_scale(input_tokens, EPS_ROW)
    normed = input_tokens * scale
    projected = jnp.einsum(
        "tsd,cdq->ctsq", normed.astype(jnp.bfloat16), weights, preferred_element_type=jnp.float32
    )
    query = split_heads(projected[0])
    query_scale = row_scale(query, EPS_HEAD)
    keyed = split_heads(projected[1])
    key_scale = row_scale(keyed, EPS_HEAD)
    values = split_heads(projected[2]).astype(jnp.bfloat16)
    return (normed, scale, query * query_scale, query_scale, keyed * key_scale, key_scale, values)


def input_gradient_rows(
    normed, scale, norm_q, q_scale, norm_k, k_scale, grad_q, grad_k, grad_v, weights
):
    query_grad = norm_back(norm_q, q_scale, grad_q).astype(jnp.bfloat16)
    key_grad = norm_back(norm_k, k_scale, grad_k).astype(jnp.bfloat16)
    stacked = jnp.stack([merge_heads(query_grad), merge_heads(key_grad), merge_heads(grad_v)])
    partial_value = jnp.einsum(
        "ctsq,cdq->tsd", stacked, weights, preferred_element_type=jnp.float32
    )
    return norm_back(normed, scale, head_totals(partial_value))


def shards(
    tokens,
    cotangent,
    hour_of,
    adjacency,
    temporal_query_key_value,
    time_out,
    spatial_query_key_value,
    space_out,
):
    rows = tokens.shape[0]
    local_hours = lax.dynamic_slice_in_dim(hour_of, lax.axis_index("hour") * rows, rows)
    input_tokens = tokens.astype(jnp.float32)
    (
        temporal_normalised,
        temporal_scale,
        temporal_query,
        temporal_query_scale,
        temporal_key,
        temporal_key_scale,
        temporal_value,
    ) = project_normalised_rows(input_tokens, temporal_query_key_value)
    query_low = temporal_query.astype(jnp.bfloat16)
    key_low = temporal_key.astype(jnp.bfloat16)
    key_all, value_all = (
        lax.all_gather(merge_heads(key_low), "hour", axis=0, tiled=True),
        lax.all_gather(merge_heads(temporal_value), "hour", axis=0, tiled=True),
    )
    key_all = split_heads(key_all)
    value_all = split_heads(value_all)
    visible = hour_of[None, :] <= local_hours[:, None]
    scores = (
        jnp.einsum("ishd,jshd->shij", query_low, key_all, preferred_element_type=jnp.float32)
        * SCORE_SCALE
    )
    weights = jnp.where(visible, jnp.exp(scores), 0.0)
    totals = jnp.sum(weights, axis=-1, keepdims=True)
    probs = weights / totals
    probs_low = probs.astype(jnp.bfloat16)
    attended = jnp.einsum(
        "shij,jshd->ishd", probs_low, value_all, preferred_element_type=jnp.float32
    ).astype(jnp.bfloat16)
    mixed = jnp.einsum(
        "isq,qd->isd", merge_heads(attended), time_out, preferred_element_type=jnp.float32
    )
    hidden_state = lax.optimization_barrier(
        (input_tokens + head_totals(mixed)).astype(jnp.bfloat16)
    ).astype(jnp.float32)
    (
        spatial_normalised,
        spatial_scale,
        spatial_query,
        spatial_query_scale,
        spatial_key,
        spatial_key_scale,
        spatial_value,
    ) = project_normalised_rows(hidden_state, spatial_query_key_value)
    grad_out = jnp.einsum(
        "isd,qd->isq", cotangent, space_out, preferred_element_type=jnp.float32
    ).astype(jnp.bfloat16)
    query_near, key_near, value_near, grad_near = (
        lax.all_to_all(
            merge_heads(spatial_query.astype(jnp.bfloat16)),
            "cluster",
            split_axis=0,
            concat_axis=1,
            tiled=True,
        ),
        lax.all_to_all(
            merge_heads(spatial_key.astype(jnp.bfloat16)),
            "cluster",
            split_axis=0,
            concat_axis=1,
            tiled=True,
        ),
        lax.all_to_all(
            merge_heads(spatial_value), "cluster", split_axis=0, concat_axis=1, tiled=True
        ),
        lax.all_to_all(grad_out, "cluster", split_axis=0, concat_axis=1, tiled=True),
    )
    query_near = split_heads(query_near)
    key_near = split_heads(key_near)
    value_near = split_heads(value_near)
    grad_near = split_heads(grad_near)
    block = jnp.arange(S) // SBLK
    listed = jnp.sum(
        (adjacency[:, :, None] == jnp.arange(NSB)[None, None, :]).astype(jnp.float32), axis=1
    )
    member = (block[:, None] == jnp.arange(NSB)[None, :]).astype(jnp.float32)
    near = jnp.dot(jnp.dot(member, listed), member.T) > 0.5
    scores_two = (
        jnp.einsum("rihd,rjhd->rhij", query_near, key_near, preferred_element_type=jnp.float32)
        * SCORE_SCALE
    )
    weights_two = jnp.where(near, jnp.exp(scores_two), 0.0)
    probs_two = weights_two / jnp.sum(weights_two, axis=-1, keepdims=True)
    dprob_two = jnp.einsum(
        "rihd,rjhd->rhij", grad_near, value_near, preferred_element_type=jnp.float32
    )
    delta_two = jnp.sum(probs_two * dprob_two, axis=-1, keepdims=True)
    dscore_two = (probs_two * (dprob_two - delta_two) * SCORE_SCALE).astype(jnp.bfloat16)
    dquery_near = jnp.einsum(
        "rhij,rjhd->rihd", dscore_two, key_near, preferred_element_type=jnp.float32
    ).astype(jnp.bfloat16)
    dkey_near = jnp.einsum(
        "rhij,rihd->rjhd", dscore_two, query_near, preferred_element_type=jnp.float32
    ).astype(jnp.bfloat16)
    dvalue_near = jnp.einsum(
        "rhij,rihd->rjhd",
        probs_two.astype(jnp.bfloat16),
        grad_near,
        preferred_element_type=jnp.float32,
    ).astype(jnp.bfloat16)
    spatial_query_gradient, spatial_key_gradient, spatial_value_gradient = (
        lax.all_to_all(
            merge_heads(dquery_near), "cluster", split_axis=1, concat_axis=0, tiled=True
        ),
        lax.all_to_all(merge_heads(dkey_near), "cluster", split_axis=1, concat_axis=0, tiled=True),
        lax.all_to_all(
            merge_heads(dvalue_near), "cluster", split_axis=1, concat_axis=0, tiled=True
        ),
    )
    hidden_state_gradient = cotangent.astype(jnp.float32) + input_gradient_rows(
        spatial_normalised,
        spatial_scale,
        spatial_query,
        spatial_query_scale,
        spatial_key,
        spatial_key_scale,
        split_heads(spatial_query_gradient).astype(jnp.float32),
        split_heads(spatial_key_gradient).astype(jnp.float32),
        split_heads(spatial_value_gradient),
        spatial_query_key_value,
    )
    grad_low = hidden_state_gradient.astype(jnp.bfloat16)
    grad_one = split_heads(
        jnp.einsum("isd,qd->isq", grad_low, time_out, preferred_element_type=jnp.float32).astype(
            jnp.bfloat16
        )
    )
    dprob = jnp.einsum("ishd,jshd->shij", grad_one, value_all, preferred_element_type=jnp.float32)
    delta = jnp.sum(probs * dprob, axis=-1, keepdims=True)
    dscore = (probs * (dprob - delta) * SCORE_SCALE).astype(jnp.bfloat16)
    temporal_query_gradient = jnp.einsum(
        "shij,jshd->ishd", dscore, key_all, preferred_element_type=jnp.float32
    )
    key_part = jnp.einsum("shij,ishd->jshd", dscore, query_low, preferred_element_type=jnp.float32)
    value_part = jnp.einsum(
        "shij,ishd->jshd", probs_low, grad_one, preferred_element_type=jnp.float32
    )
    summed = lax.psum_scatter(
        jnp.concatenate([merge_heads(key_part), merge_heads(value_part)], axis=-1).astype(
            jnp.bfloat16
        ),
        "hour",
        scatter_dimension=0,
        tiled=True,
    ).astype(jnp.float32)
    half_width = summed.shape[-1] // 2
    temporal_key_gradient = split_heads(summed[..., :half_width])
    temporal_value_gradient = split_heads(summed[..., half_width:])
    input_gradient_total = input_gradient_rows(
        temporal_normalised,
        temporal_scale,
        temporal_query,
        temporal_query_scale,
        temporal_key,
        temporal_key_scale,
        temporal_query_gradient,
        temporal_key_gradient,
        temporal_value_gradient.astype(jnp.bfloat16),
        temporal_query_key_value,
    )
    return (hidden_state_gradient + input_gradient_total).astype(jnp.bfloat16)


NT = (((1,), (1,)), ((), ()))


def dot(a, b):
    return jnp.dot(a, b, preferred_element_type=jnp.float32)


def dot_nt(a, b):
    return lax.dot_general(a, b, NT, preferred_element_type=jnp.float32)


def low(values):
    return values.astype(jnp.bfloat16)


def layer_kernel(
    cfg,
    tok_in,
    cot_in,
    hour_row,
    adj,
    w1,
    wo1,
    w2,
    wo2,
    out,
    rawt,
    rawc,
    tok,
    cot,
    tokT,
    tokS,
    cotS,
    w1v,
    w1T,
    w2T,
    woT,
    woF,
    w2F,
    wsF,
    nrm,
    qT1,
    kT1,
    r1q,
    r1k,
    qTb1,
    kb1,
    kTb1,
    vb1,
    vTb1,
    E1,
    li1,
    oT1,
    dqT1,
    dkT1,
    dvT1,
    o1buf,
    o1S,
    qT2,
    kT2,
    r2T,
    qTb2,
    kb2,
    kTb2,
    vb2,
    gT2,
    dqT2,
    dkT2,
    dvT2,
    g1buf,
    g1T,
    dhs,
    dhO,
    psend,
    precv,
    pown,
    g3,
    t1s,
    t1O,
    loc_sem,
    z_send,
    z_recv,
    f_send,
    f_recv,
    x_send,
    x_recv,
    w_send,
    w_recv,
    o_send,
    o_recv,
    g_send,
    g_recv,
    d_send,
    d_recv,
    p_send,
    p_recv,
    t_send,
    t_recv,
    e_send,
    e_recv,
):
    NH, NC, RW, D, W = cfg
    HL = W // HS
    HB = NC * RW
    BLK = 2 * HB
    NT1 = NH * BLK
    NS = NC * NH
    U = 2
    RU = RW // U
    N2 = NS * RU
    QU = NT1 // U
    hr = lax.axis_index("hour")
    cl = lax.axis_index("cluster")
    m = lax.axis_index("mp")
    sib = 1 - m
    offsets = [
        (a % NH, b % NC, c)
        for a in (2, 1, *range(3, NH + 1))
        for b in range(1, NC + 1)
        for c in range(2)
        if (a % NH, b % NC, c) != (0, 0, 0)
    ]

    def peer(off):
        return (lax.rem(hr + off[0], NH), lax.rem(cl + off[1], NC), lax.rem(m + off[2], 2))

    def ids(p):
        return {"hour": p[0], "cluster": p[1], "mp": p[2]}

    def remote(src, dst, ss, rs, dev):
        return pltpu.make_async_remote_copy(
            src_ref=src,
            dst_ref=dst,
            send_sem=ss,
            recv_sem=rs,
            device_id=dev,
            device_id_type=pl.DeviceIdType.MESH,
        )

    barrier = pltpu.get_barrier_semaphore()
    for off in offsets:
        pl.semaphore_signal(
            barrier, inc=1, device_id=ids(peer(off)), device_id_type=pl.DeviceIdType.MESH
        )

    halves = []
    for c, half in enumerate((m, sib)):
        halves.append([])
        for b in range(NC):
            span = pl.ds((2 * b + half) * RW, RW)
            halves[c].append(
                pltpu.make_async_copy(tok_in.at[span], rawt.at[span], loc_sem.at[6 + c * NC + b])
            )
    local = halves[0] + [
        pltpu.make_async_copy(w1, w1v, loc_sem.at[1]),
        pltpu.make_async_copy(cot_in, rawc, loc_sem.at[2]),
        pltpu.make_async_copy(wo1, woF.at[m], loc_sem.at[3]),
        pltpu.make_async_copy(w2, w2F.at[m], loc_sem.at[4]),
        pltpu.make_async_copy(wo2, wsF.at[m], loc_sem.at[5]),
    ]
    local[NC:NC] = halves[1]
    for copy in local:
        copy.start()
    local = [None] + local[2 * NC :]

    def by_token(raw, rows_of):
        x = jnp.transpose(raw[...], (1, 0, 2))
        for b in range(NC):
            for c in range(2):
                first = (2 * b + c) * RW
                rows_of[:, c, b * RW : (b + 1) * RW] = x[:, first : first + RW]

    def half_by_token(c, half):
        for b in range(NC):
            halves[c][b].wait()
            x = jnp.transpose(rawt[pl.ds((2 * b + half) * RW, RW)], (1, 0, 2))
            tok[:, half, b * RW : (b + 1) * RW] = x

    half_by_token(0, m)
    tokS[cl] = tok[:, m, pl.ds(cl * RW, RW)]
    pl.semaphore_wait(barrier, len(offsets))

    zc = {}
    for a in range(1, NH):
        d = lax.rem(hr + a, NH)
        zc[a] = remote(
            tok.at[d, m], tokT.at[a, m], z_send.at[a], z_recv.at[a], ids((d, cl, m))
        )
        zc[a].start()
    xc = []

    def to_spatial(which, src, dst):
        for b in range(1, NC):
            dc = lax.rem(cl + b, NC)
            copy = remote(
                src.at[:, m, pl.ds(dc * RW, RW), :],
                dst.at[cl],
                x_send.at[which, b],
                x_recv.at[which, b],
                ids((hr, dc, m)),
            )
            copy.start()
            xc.append(copy)

    to_spatial(0, tok, tokS)
    half_by_token(1, sib)
    tokT[0] = tok[hr]
    wc = []
    for which, (src, dst) in enumerate(((wo1, woF), (w2, w2F), (wo2, wsF))):
        copy = remote(src, dst.at[m], w_send.at[which], w_recv.at[which], ids((hr, cl, sib)))
        copy.start()
        wc.append(copy)

    def head_norm(pT, heads):
        n = pT.shape[-1]
        p3 = pT.reshape(heads, HS, n)
        r = lax.rsqrt(jnp.mean(p3 * p3, axis=1, keepdims=True) + EPS_HEAD)
        return p3 * r, r

    def row_norm(x):
        r = lax.rsqrt(jnp.mean(x * x, axis=-1, keepdims=True) + EPS_ROW)
        return x * r, r

    local[2].wait()
    by_token(rawc, cot)
    cotS[cl] = cot[:, m, pl.ds(cl * RW, RW)]
    to_spatial(1, cot, cotS)
    local[1].wait()
    local[4].wait()
    for c in range(3):
        w1T[c * W : (c + 1) * W] = w1v[c].T
        w2T[m, c] = w2F[m, c].T
    fc = {}

    hours = jnp.concatenate(
        [hour_row[pl.ds(lax.rem(hr + NH - a, NH), 1), :] for a in range(NH)], axis=1
    ).astype(jnp.float32)
    place = lax.broadcasted_iota(jnp.int32, (1, NT1), 1) % BLK // RW
    hours = jnp.where(
        place == 1,
        pltpu.roll(hours, NT1 - RW, 1),
        jnp.where(place == 2, pltpu.roll(hours, RW, 1), hours),
    )
    hours = jnp.broadcast_to(hours, (128, NT1)).T
    hours_j = hours[:, :1]
    hours = hours.reshape(NT1 // RW, U, RU, 128)
    hours_i = [hours[:, u].reshape(QU, 128).T[:1] for u in range(U)]
    factor = SCORE_SCALE * LOG2E

    def forward(a):
        zc[a].wait_recv()
        half = tokT.at[a, m]
        fc[a] = remote(half, half, f_send.at[a], f_recv.at[a], ids((hr, cl, sib)))
        fc[a].start()

    def project_queries(u, p):
        pair = slice(p * BLK, (p + 1) * BLK)
        rows = nrm[2 * p : 2 * p + 2, :, u].reshape(BLK, D)
        q, rq = head_norm(dot(rows, w1v[0]).T, HL)
        qT1[u, :, :, pair] = q
        qTb1[u, :, :, pair] = low(q)
        r1q[u, :, :, pair] = rq

    for a in range(NH):
        if a == 1:
            wc[1].wait_recv()
            for c in range(3):
                w2T[sib, c] = w2F[sib, c].T
            local[3].wait()
            wc[0].wait_recv()
            for half in range(2):
                woT[:, half * W : (half + 1) * W] = woF[half].T
            forward(1)
        if 0 < a < NH - 1:
            forward(a + 1)
        if a > 0:
            fc[a].wait_recv()
        x = tokT[a].reshape(BLK, D).astype(jnp.float32)
        n, _ = row_norm(x)
        n = low(n)
        nrm[a] = n.reshape(2 * NC, U, RU, D)
        cols = slice(a * BLK, (a + 1) * BLK)
        k, rk = head_norm(dot(n, w1v[1]).T, HL)
        kT1[:, :, cols] = k
        kTb1[:, :, cols] = low(k)
        r1k[:, :, cols] = rk
        kn = low(k).reshape(W, BLK).T
        v = low(dot(n, w1v[2]))
        vTb1[:, :, cols] = v.T.reshape(HL, HS, BLK)
        for h in range(HL):
            kb1[h, cols, :] = kn[:, h * HS : (h + 1) * HS]
            vb1[h, cols, :] = v[:, h * HS : (h + 1) * HS]
        if a % 2:
            for u in range(U if a < NH - 1 else 1):
                project_queries(u, a // 2)

    oc = []
    for u in range(U):
        if u > 0:
            project_queries(u, NH // 2 - 1)
        for h in range(HL):
            e = jnp.where(
                hours_j <= hours_i[u], jnp.exp2(dot(kb1[h], qTb1[u, h]) * factor), 0.0
            )
            li1[u, h] = 1.0 / jnp.sum(e, axis=0, keepdims=True)
            E1[u, h] = low(e)
        for h in range(HL):
            oT1[u, h] = dot(vTb1[h], E1[u, h]) * li1[u, h]
        o1buf[u] = low(oT1[u]).reshape(W, QU).T.reshape(NH, 2, NC, RU, W)
        oc.append([])
        for t, off in enumerate(offsets):
            p = peer(off)
            copy = remote(
                o1buf.at[u, (NH - off[0]) % NH, p[2], p[1]],
                o1S.at[u, m, cl * NH + hr],
                o_send.at[u, t],
                o_recv.at[u, t],
                ids(p),
            )
            copy.start()
            oc[u].append(copy)
        o1S.at[u][m, cl * NH + hr] = o1buf[u, 0, m, cl]

    local[5].wait()
    for copy in xc:
        copy.wait_recv()
    wc[2].wait_recv()
    for copy in list(zc.values()) + list(fc.values()) + xc + wc:
        copy.wait_send()
    for u in range(U):
        cot2 = cotS[:, :, u * RU : (u + 1) * RU].reshape(N2, D)
        for half in range(2):
            gT2[u, half * HL : (half + 1) * HL] = low(dot_nt(wsF[half], cot2)).reshape(HL, HS, N2)
    rows = lax.broadcasted_iota(jnp.int32, (N2, N2), 0)
    columns = lax.broadcasted_iota(jnp.int32, (N2, N2), 1)
    per_block = SBLK * RU
    block_j = rows // per_block
    block_i = columns // per_block
    near = rows < 0
    for b in range(NSB):
        for c in range(adj.shape[0]):
            near = near | ((block_i == b) & (block_j == adj[c, b]))
    near = near & (rows % RU == columns % RU)
    near = near.astype(jnp.float32)

    def head_back(nT, r, dT):
        return r * (dT - nT * jnp.mean(nT * dT, axis=1, keepdims=True))

    gc, dc_copies = [[] for u in range(U)], []
    for u in range(U):
        span = pl.ds(u * RU, RU)
        for copy in oc[u]:
            copy.wait_recv()
        hid = tokS[:, :, u * RU : (u + 1) * RU].reshape(N2, D).astype(jnp.float32)
        o1 = jnp.concatenate([o1S[u, half].reshape(N2, W) for half in range(2)], axis=-1)
        hid = hid + dot(o1, woF[...].reshape(2 * W, D))
        hid = low(hid).astype(jnp.float32)
        n2f, r2 = row_norm(hid)
        n2 = low(n2f)
        for half in range(2):
            hs = slice(half * HL, (half + 1) * HL)
            q, rq = head_norm(dot(n2, w2F[half, 0]).T, HL)
            qT2[hs] = q
            qTb2[hs] = low(q)
            r2T[0, hs] = rq
            k, rk = head_norm(dot(n2, w2F[half, 1]).T, HL)
            kT2[hs] = k
            kTb2[hs] = low(k)
            r2T[1, hs] = rk
            kn = low(k).reshape(W, N2).T
            v = low(dot(n2, w2F[half, 2]))
            for h in range(HL):
                kb2[half * HL + h] = kn[:, h * HS : (h + 1) * HS]
                vb2[half * HL + h] = v[:, h * HS : (h + 1) * HS]

        probs, grads = [], []
        for h in range(2 * HL):
            e = near * jnp.exp2(dot(kb2[h], qTb2[h]) * factor)
            probs.append(e * (1.0 / jnp.sum(e, axis=0, keepdims=True)))
        for h in range(2 * HL):
            p, dp = probs[h], dot(vb2[h], gT2[u, h])
            dl = jnp.sum(p * dp, axis=0, keepdims=True)
            grads.append(low(p * (dp - dl) * SCORE_SCALE))
        for h in range(2 * HL):
            dvT2[h] = low(dot_nt(gT2[u, h], low(probs[h])))
        for h in range(2 * HL):
            dqT2[h] = dot(kTb2[h], grads[h])
            dkT2[h] = dot_nt(qTb2[h], grads[h])

        grads = []
        for half in range(2):
            hs = slice(half * HL, (half + 1) * HL)
            dq = low(head_back(qT2[hs], r2T[0, hs], dqT2[hs])).reshape(W, N2).T
            dk = low(head_back(kT2[hs], r2T[1, hs], dkT2[hs])).reshape(W, N2).T
            grads += [dq, dk, dvT2[hs].reshape(W, N2).T]
        dn2 = dot(jnp.concatenate(grads, axis=-1), w2T[...].reshape(6 * W, D))
        dh = cotS[:, :, u * RU : (u + 1) * RU].reshape(N2, D).astype(jnp.float32) + r2 * (
            dn2 - n2f * jnp.mean(n2f * dn2, axis=-1, keepdims=True)
        )
        dhb = low(dh)
        g1 = low(dot(dhb, woT[...]))
        for half in range(2):
            g1buf[u, half] = g1[:, half * W : (half + 1) * W].reshape(NS, RU, W)

        for t, off in enumerate(offsets):
            p = peer(off)
            copy = remote(
                g1buf.at[u, p[2], p[1] * NH + p[0]],
                g1T.at[u, off[0], m, cl],
                g_send.at[u, t],
                g_recv.at[u, t],
                ids(p),
            )
            copy.start()
            gc[u].append(copy)
        g1T[u, 0, m, cl] = g1buf.at[u][m, cl * NH + hr]
        dhs[:, :, u * RU : (u + 1) * RU] = dhb.reshape(NC, NH, RU, D)

    for copy in sum(oc, []):
        copy.wait_send()
    for u in range(U):
        for copy in gc[u]:
            copy.wait_recv()
        if u == U - 1:
            for b in range(1, NC):
                dc = lax.rem(cl + b, NC)
                copy = remote(
                    dhs.at[dc], dhO.at[cl], d_send.at[b], d_recv.at[b], ids((hr, dc, m))
                )
                copy.start()
                dc_copies.append(copy)
            dhO[cl] = dhs[cl]
        gT = g1T[u].reshape(QU, W).T.reshape(HL, HS, QU).astype(jnp.float32)
        gs = gT * (SCORE_SCALE * li1[u])
        dl = jnp.sum(oT1[u] * gs, axis=1, keepdims=True)
        gs = low(gs)
        ds = []
        for h in range(HL):
            dp = dot(vb1[h], gs[h])
            ds.append(low(E1[u, h].astype(jnp.float32) * (dp - dl[h])))
        for h in range(HL):
            dv = dot_nt(gs[h], E1[u, h])
            dvT1[h] = dv if u == 0 else dvT1[h] + dv
        for h in range(HL):
            dqT1[u, h] = dot(kTb1[h], ds[h])
            dk = dot_nt(qTb1[u, h], ds[h])
            dkT1[h] = dk if u == 0 else dkT1[h] + dk
        dq = low(head_back(qT1[u], r1q[u], dqT1[u])).reshape(W, QU).T
        g3[:, :, :, u, :, :W] = dq.reshape(NH, 2, NC, RU, W)
    dk = low(head_back(kT1[...], r1k[...], dkT1[...])).reshape(W, NT1).T
    dv = low(dvT1[...] * (1.0 / SCORE_SCALE)).reshape(W, NT1).T
    g3[..., W : 2 * W] = dk.reshape(NH, 2, NC, U, RU, W)
    g3[..., 2 * W :] = dv.reshape(NH, 2, NC, U, RU, W)

    def partial(which, span):
        rows = g3[span, which].reshape(-1, 3 * W)
        return dot(rows, w1T[...]).reshape(-1, HB, D)

    pc, tc = {}, {}
    spans = [slice(first, first + 2) for first in range(NH - 2, -1, -2)]
    for span in spans:
        psend[span] = low(partial(sib, span))
        for a in range(span.stop - 1, span.start - 1, -1):
            pc[a] = remote(
                psend.at[a], precv.at[a], p_send.at[a], p_recv.at[a], ids((hr, cl, sib))
            )
            pc[a].start()
    for span in spans:
        pown[span] = partial(m, span)
        for a in range(span.stop - 1, span.start - 1, -1):
            pc[a].wait_recv()
            dn1 = pown[a] + precv[a].astype(jnp.float32)
            n1f, r1 = row_norm(tokT[a, m].astype(jnp.float32))
            t1 = low(r1 * (dn1 - n1f * jnp.mean(n1f * dn1, axis=-1, keepdims=True)))
            if a == 0:
                t1O[hr] = t1
                continue
            t1s[a] = t1
            d = lax.rem(hr + NH - a, NH)
            for b in range(NC):
                rows = pl.ds(b * RW, RW)
                tc[a, b] = remote(
                    t1s.at[a, rows],
                    t1O.at[hr, rows],
                    t_send.at[a, b],
                    t_recv.at[a, b],
                    ids((d, cl, m)),
                )
                tc[a, b].start()
    for copy in dc_copies:
        copy.wait_recv()
    for copy in sum(gc, []) + dc_copies + list(pc.values()):
        copy.wait_send()
    ec = []
    for b in range(NC):
        for a in range(NH - 1, 0, -1):
            tc[a, b].wait_recv()
        mine = t1O[:, b * RW : (b + 1) * RW].astype(jnp.float32) + dhO[b].astype(jnp.float32)
        place = pl.ds((2 * b + m) * RW, RW)
        out[place] = jnp.transpose(low(mine), (1, 0, 2))
        copy = remote(
            out.at[place], out.at[place], e_send.at[b], e_recv.at[b], ids((hr, cl, sib))
        )
        copy.start()
        ec.append(copy)

    for copy in tc.values():
        copy.wait_send()
    for copy in ec:
        copy.wait()


def fast_shards(
    mesh,
    tokens,
    cotangent,
    hour_of,
    adjacency,
    temporal_query_key_value,
    time_out,
    spatial_query_key_value,
    space_out,
):
    NH, NC = mesh.shape["hour"], mesh.shape["cluster"]
    rows, SL, D = tokens.shape
    W = time_out.shape[0]
    RW = rows // (2 * NC)
    HB = NC * RW
    NT1 = NH * rows
    NS = NC * NH
    U = 2
    RU = RW // U
    N2 = NS * RU
    QU = NT1 // U
    HL = W // HS
    NO = 2 * NH * NC - 1

    bf, f32 = jnp.bfloat16, jnp.float32
    V = pltpu.VMEM
    dma = pltpu.SemaphoreType.DMA
    hbm = pl.BlockSpec(memory_space=pl.ANY)
    return pl.pallas_call(
        functools.partial(layer_kernel, (NH, NC, RW, D, W)),
        out_shape=pltpu.VMEM((rows, SL, D), bf),
        in_specs=[
            hbm,
            hbm,
            pl.BlockSpec(memory_space=pltpu.VMEM),
            pl.BlockSpec(memory_space=pltpu.SMEM),
            hbm,
            hbm,
            hbm,
            hbm,
        ],
        out_specs=pl.BlockSpec(memory_space=pltpu.VMEM),
        scratch_shapes=[
            V((rows, SL, D), bf),
            V((rows, SL, D), bf),
            V((SL, 2, HB, D), bf),
            V((SL, 2, HB, D), bf),
            V((NH, 2, HB, D), bf),
            V((NC, NH, RW, D), bf),
            V((NC, NH, RW, D), bf),
            V((3, D, W), bf),
            V((3 * W, D), bf),
            V((2, 3, W, D), bf),
            V((D, 2 * W), bf),
            V((2, W, D), bf),
            V((2, 3, D, W), bf),
            V((2, W, D), bf),
            V((NH, 2 * NC, U, RU, D), bf),
            V((U, HL, HS, QU), f32),
            V((HL, HS, NT1), f32),
            V((U, HL, 1, QU), f32),
            V((HL, 1, NT1), f32),
            V((U, HL, HS, QU), bf),
            V((HL, NT1, HS), bf),
            V((HL, HS, NT1), bf),
            V((HL, NT1, HS), bf),
            V((HL, HS, NT1), bf),
            V((U, HL, NT1, QU), bf),
            V((U, HL, 1, QU), f32),
            V((U, HL, HS, QU), f32),
            V((U, HL, HS, QU), f32),
            V((HL, HS, NT1), f32),
            V((HL, HS, NT1), f32),
            V((U, NH, 2, NC, RU, W), bf),
            V((U, 2, NS, RU, W), bf),
            V((2 * HL, HS, N2), f32),
            V((2 * HL, HS, N2), f32),
            V((2, 2 * HL, 1, N2), f32),
            V((2 * HL, HS, N2), bf),
            V((2 * HL, N2, HS), bf),
            V((2 * HL, HS, N2), bf),
            V((2 * HL, N2, HS), bf),
            V((U, 2 * HL, HS, N2), bf),
            V((2 * HL, HS, N2), f32),
            V((2 * HL, HS, N2), f32),
            V((2 * HL, HS, N2), bf),
            V((U, 2, NS, RU, W), bf),
            V((U, NH, 2, NC, RU, W), bf),
            V((NC, NH, RW, D), bf),
            V((NC, NH, RW, D), bf),
            V((NH, HB, D), bf),
            V((NH, HB, D), bf),
            V((NH, HB, D), f32),
            V((NH, 2, NC, U, RU, 3 * W), bf),
            V((NH, HB, D), bf),
            V((NH, HB, D), bf),
            dma((6 + 2 * NC,)),
            dma((NH,)),
            dma((NH,)),
            dma((NH,)),
            dma((NH,)),
            dma((2, NC)),
            dma((2, NC)),
            dma((3,)),
            dma((3,)),
            dma((U, NO)),
            dma((U, NO)),
            dma((U, NO)),
            dma((U, NO)),
            dma((NC,)),
            dma((NC,)),
            dma((NH,)),
            dma((NH,)),
            dma((NH, NC)),
            dma((NH, NC)),
            dma((NC,)),
            dma((NC,)),
        ],
        compiler_params=pltpu.CompilerParams(
            collective_id=0, has_side_effects=True, vmem_limit_bytes=58 << 20
        ),
        name="layer",
    )(
        tokens,
        cotangent,
        hour_of.reshape(NH, rows),
        adjacency.T,
        temporal_query_key_value,
        time_out,
        spatial_query_key_value,
        space_out,
    )


def fits(mesh, tokens):
    NH, NC = mesh.shape["hour"], mesh.shape["cluster"]
    SL = tokens.shape[1] // NC
    rows = tokens.shape[0] // (mesh.shape["group"] * NH)
    return (
        mesh.shape["mp"] == 2
        and SL == NH
        and NC == 2
        and NC * NH == S
        and rows % 128 == 0
        and (rows // (2 * NC)) % 32 == 0
        and NH * rows <= 512
    )


def solution(mesh):
    def run(*args):
        body = functools.partial(fast_shards, mesh) if fits(mesh, args[0]) else shards
        return jax.shard_map(
            body,
            mesh=mesh,
            in_specs=(
                P(("group", "hour"), "cluster", None),
                P(("group", "hour"), "cluster", None),
                P("group"),
                P(),
                P(None, None, "mp"),
                P("mp", None),
                P(None, None, "mp"),
                P("mp", None),
            ),
            out_specs=P(("group", "hour"), "cluster", None),
            check_vma=False,
        )(*args)

    return run
```
